512 devices in a mesh: space: 32 (over z_hi, x, y), tm: 16 (over z_lo, core).
Axes of the slice: x: 4, y: 4, z: 16 (z_hi: 2, z_lo: 8; z = z_hi * 8 + z_lo), core: 2. Of those that a mesh axis runs over, the one named last changes fastest.
Arguments:
- concentration: float32 [64, 128, 128], P('space'), may hold values from 0 to 2
- velocity: bfloat16 [3, 64, 128, 128], P(None, 'space'), may hold values from -0.29882812 to 0.29882812
- porosity: float32 [64, 128, 128], P('space'), may hold values from 0.15 to 0.4
- contacts: int32 [512, 4], P('space'), may hold values from 0 to 32767
- sources: int32 [32, 2], P('tm'), may hold values from 0 to 511
- receivers: int32 [32, 64, 2], P('tm'), may hold values from 0 to 511, all different within a row
- observed: float32 [32, 64], P('tm'), may hold values from -6 to 6
- potential_init: float32 [32, 64, 128, 128], P('tm', 'space'), may hold values from -12 to 12
- adjoint_init: float32 [32, 64, 128, 128], P('tm', 'space'), may hold values from -12 to 12
Outputs:
- gradient: float32 [64, 128, 128], P('space')
- readings: float32 [32, 64], P('tm')
The draws below stay inside these ranges and needn't reach their ends.
Inputs may be any that keep to these rules, and one draw needn't show every extreme that they name: contacts[e, c] indexes the flattened cells of tile e // 16, which holds electrode e. `sources`: electrode ids. `receivers`: the two electrodes of a receiver pair differ.
All inputs are finite; a program needn't handle non-finite values.
Results may differ from the reference program's by a relative error of at most 0.0003.
Values sent between devices are 32-bit elements; how exact they have to be, the bound alone decides.
A program may use at most 64 MiB of HBM per device.

```python
import math
import jax
import jax.numpy as jnp
from jax import lax

CX = 2
NY = 128
NZ = 128
E_DEV = 16
RECEIVER_PAIRS = 64
CONTACTS = 4
STEPS = 8
RELAX_SWEEPS = 6
NX = 64
ELECTRODE_COUNT = 512
SURVEY_TIMES = 32


def set_ends(values, own_key, low, top_value):
    longest = values.shape.index(max(values.shape))
    spots = []
    for shift in (0, 1):
        where = [jax.random.randint(jax.random.fold_in(own_key, axis), (), 0, length) for axis, length in enumerate(values.shape)]
        where[longest] = (where[longest] + shift) % values.shape[longest]
        spots.append(tuple(where))
    return values.at[spots[0]].set(low).at[spots[1]].set(top_value)


def levels(key, shape, shards, least, largest):
    def one(position, shards_of):
        draws = jax.random.uniform(jax.random.fold_in(jax.random.fold_in(key, 6), position), (shards_of,), jnp.float32, least / len(shards), largest / len(shards))
        return jnp.repeat(jnp.exp(draws), shape[position] // shards_of).reshape((-1,) + (1,) * (len(shape) - position - 1))

    level = one(*shards[0])
    for cut in shards[1:]:
        level = level * one(*cut)
    return level


def distinct(own_key, rows, number_of, top, lift):
    sequence = jax.random.permutation(jax.random.fold_in(own_key, 1), number_of)
    pull = sequence
    for power in range(3):
        pull = pull * pull // number_of
    pull = pull * lift // number_of
    lots = jax.random.randint(jax.random.fold_in(own_key, 2), (rows, number_of), 0, 4096) + pull
    fixed_rows = jax.random.permutation(jax.random.fold_in(own_key, 3), rows)[jnp.arange(number_of) % rows]
    lots = jnp.where(jnp.arange(rows)[:, None] == fixed_rows[None, :], 1 << 14, lots)
    merit = lots * number_of + jnp.arange(number_of)
    return lax.top_k(merit.astype(jnp.int32), top)[1].astype(jnp.int32)


def bell_draw(own_key, dims, width, most, cuts=(), kind=jnp.bfloat16):
    gain = levels(own_key, dims, cuts, -0.22, 0.18) if cuts else 1.0
    values = jax.random.normal(own_key, dims, jnp.float32) * width * gain
    return jnp.minimum(jnp.maximum(values, -most), most).astype(kind)


def setup_inputs(seed: int = 0) -> dict:
    key_of = jax.random.split(jax.random.key(seed), 10)
    return {
        "concentration": jnp.clip(2.0 * jax.random.uniform(key_of[0], (NX, NY, NZ), jnp.float32) ** levels(key_of[0], (NX, NY, NZ), ((0, 32),), -0.2, 0.2), 0.0, 2.0),
        "velocity": jnp.clip(jax.random.uniform(key_of[1], (3, NX, NY, NZ), jnp.float32, -0.29882812, 0.29882812) * levels(key_of[1], (3, NX, NY, NZ), ((1, 32),), -0.4, 0.0), -0.29882812, 0.29882812).astype(jnp.bfloat16),
        "porosity": jnp.clip(jnp.exp(math.log(0.4) - 0.98082923 * jax.random.uniform(key_of[2], (NX, NY, NZ), jnp.float32) ** levels(key_of[2], (NX, NY, NZ), ((0, 32),), -0.2, 0.2)), 0.15, 0.4),
        "contacts": set_ends(jax.random.randint(key_of[3], (ELECTRODE_COUNT, CONTACTS), 0, CX * NY * NZ), jax.random.fold_in(key_of[3], 1), 0, (CX * NY * NZ) - 1).astype(jnp.int32),
        "sources": set_ends(jax.random.randint(key_of[4], (SURVEY_TIMES, 2), 0, ELECTRODE_COUNT), jax.random.fold_in(key_of[4], 1), 0, ELECTRODE_COUNT - 1).astype(jnp.int32),
        "receivers": distinct(key_of[5], SURVEY_TIMES * RECEIVER_PAIRS, ELECTRODE_COUNT, 2, 0).reshape((SURVEY_TIMES, RECEIVER_PAIRS, 2)),
        "observed": bell_draw(key_of[6], (SURVEY_TIMES, RECEIVER_PAIRS), 1.0, 6.0, ((0, 16),), jnp.float32),
        "potential_init": bell_draw(key_of[7], (SURVEY_TIMES, NX, NY, NZ), 2.0, 12.0, ((0, 16), (1, 32)), jnp.float32),
        "adjoint_init": bell_draw(key_of[8], (SURVEY_TIMES, NX, NY, NZ), 2.0, 12.0, ((0, 16), (1, 32)), jnp.float32),
    }


archie_exponent = 1.8
water_conductivity = 0.5
relaxation = 0.8
injected_current = 4.0


def behind(values, along):
    widths = [(0, 0)] * values.ndim
    widths[along] = (1, 0)
    return lax.slice_in_dim(jnp.pad(values, widths), 0, values.shape[along], axis=along)


def beyond(values, along):
    widths = [(0, 0)] * values.ndim
    widths[along] = (0, 1)
    return lax.slice_in_dim(jnp.pad(values, widths), 1, values.shape[along] + 1, axis=along)


def harmonic(first, second):
    return 2.0 * (first * second) / (first + second)


def reference(concentration, velocity, porosity, contacts, sources, receivers, observed, potential_init, adjoint_init):
    speeds = velocity.astype(jnp.float32)
    tracer = concentration
    for _ in range(STEPS):
        change = jnp.zeros_like(tracer)
        for dim_index in range(3):
            speed = speeds[dim_index]
            change = change + jnp.maximum(speed, 0.0) * (tracer - behind(tracer, dim_index)) + jnp.minimum(speed, 0.0) * (beyond(tracer, dim_index) - tracer)
        tracer = tracer - change
    conductivity = jnp.exp(archie_exponent * jnp.log(porosity)) * (water_conductivity + tracer)
    upper_faces = [harmonic(conductivity, beyond(conductivity, d)) for d in range(3)]
    lower_faces = [behind(upper_faces[d], d) for d in range(3)]
    diagonal_sum = upper_faces[0] + lower_faces[0] + upper_faces[1] + lower_faces[1] + upper_faces[2] + lower_faces[2]
    tiles = jnp.arange(ELECTRODE_COUNT, dtype=jnp.int32) // E_DEV
    contact_cells = (tiles[:, None] * (CX * NY * NZ) + contacts).astype(jnp.int32)
    electrode_ids = jnp.arange(ELECTRODE_COUNT, dtype=jnp.int32)

    def inject(current):
        spread = jnp.repeat(current / CONTACTS, CONTACTS)
        field = jnp.zeros((NX * NY * NZ,), jnp.float32).at[contact_cells.reshape(-1)].add(spread)
        return field.reshape(NX, NY, NZ)

    def relax_sweep(field, source):
        gathered = upper_faces[0] * beyond(field, 0) + lower_faces[0] * behind(field, 0)
        gathered = gathered + upper_faces[1] * beyond(field, 1) + lower_faces[1] * behind(field, 1)
        gathered = gathered + upper_faces[2] * beyond(field, 2) + lower_faces[2] * behind(field, 2)
        return (1.0 - relaxation) * field + relaxation * (source + gathered) / diagonal_sum

    def survey(running, survey_data):
        source_pair, receiver_pair, observed_row, potential, adjoint = survey_data
        current = injected_current * ((electrode_ids == source_pair[0]).astype(jnp.float32) - (electrode_ids == source_pair[1]).astype(jnp.float32))
        source = inject(current)
        for _ in range(RELAX_SWEEPS):
            potential = relax_sweep(potential, source)
        voltage_readings = jnp.sum(potential.reshape(-1)[contact_cells], axis=1) / CONTACTS
        readings = voltage_readings[receiver_pair[:, 0]] - voltage_readings[receiver_pair[:, 1]]
        misfit = readings - observed_row
        backward_current = jnp.zeros((ELECTRODE_COUNT,), jnp.float32).at[receiver_pair[:, 0]].add(misfit).at[receiver_pair[:, 1]].add(-misfit)
        adjoint_source = inject(backward_current)
        for _ in range(RELAX_SWEEPS):
            adjoint = relax_sweep(adjoint, adjoint_source)
        products = jnp.zeros_like(potential)
        for dim_index in range(3):
            products = products + upper_faces[dim_index] * (beyond(potential, dim_index) - potential) * (beyond(adjoint, dim_index) - adjoint)
        return running - products, readings

    gradient, readings = lax.scan(survey, jnp.zeros((NX, NY, NZ), jnp.float32), (sources, receivers, observed, potential_init, adjoint_init))
    return gradient, readings
```

```python
import jax
import jax.numpy as jnp
from jax import lax
from jax.experimental import pallas as pl
from jax.experimental.pallas import tpu as pltpu
from jax.sharding import PartitionSpec as P

STEPS = 8
RELAX_SWEEPS = 6
MESH = pl.DeviceIdType.MESH
HIGH = lax.Precision.HIGHEST
F32 = jnp.float32


def harmonic(first, second):
    return 2.0 * (first * second) / (first + second)


def iota(shape, dim):
    return lax.broadcasted_iota(jnp.int32, shape, dim)


def dot(a, b):
    return lax.dot_general(a, b, (((1,), (0,)), ((), ())), precision=HIGH, preferred_element_type=F32)


def dot_t(a, b):
    return lax.dot_general(a, b, (((1,), (1,)), ((), ())), precision=HIGH, preferred_element_type=F32)


def kernel(
    inp, pot, adj, meta, grad, read,
    ct, yct, yst, tv, sg, ysg, yss, coef, rdiag, bsrc,
    pf, ypf, ypsend, af, yaf, yasend,
    mbuf, rt, lt, vb, vsend, vall, rsend, rdin,
    gbuf, grx, gsum, rsbuf, osum,
    in_s, in_r, rel_s, t_s, t_r, sw_s, sw_r, sg_s, sg_r, tile_s, tile_r,
    p_s, p_r, a_s, a_r, v_s, v_r, rd_s, rd_r, gx_s, gx_r, rs_s, rs_r, ag_s, ag_r,
):
    space = lax.axis_index("space")
    tm = lax.axis_index("tm")
    zh = space // 16
    x = (space // 4) % 4
    y = space % 4
    zl = tm // 2
    c = tm % 2
    z = zh * 8 + zl

    def dev(x_, y_, z_, c_):
        return {"space": (z_ // 8) * 16 + x_ * 4 + y_, "tm": (z_ % 8) * 2 + c_}

    def remote(src, dst, s, r, where):
        return pltpu.make_async_remote_copy(
            src_ref=src, dst_ref=dst, send_sem=s, recv_sem=r, device_id=where, device_id_type=MESH
        )

    def arrived(ref, sem):
        pltpu.make_async_copy(ref, ref, sem).wait()

    xn = (x + 1) % 4
    xp = (x + 3) % 4
    yn = (y + 1) % 4
    yp = (y + 3) % 4
    x_last = (x + 1) // 4
    x_first = (3 - x) // 3
    y_last = (y + 1) // 4
    y_first = (3 - y) // 3

    zero_plane = jnp.zeros((32, 128), F32)

    @pl.when((x == 0) & (c == 0))
    def _():
        for par in range(2):
            ct[par, 0] = zero_plane

    @pl.when((x == 3) & (c == 1))
    def _():
        for par in range(2):
            ct[par, 9] = zero_plane

    @pl.when(x == 0)
    def _():
        sg[1, 0] = zero_plane
        for f in (pf, af):
            for par in range(2):
                f[par, 1, 0] = zero_plane

    @pl.when(x == 3)
    def _():
        sg[2, 9] = zero_plane
        for f in (pf, af):
            for par in range(2):
                f[par, 2, 9] = zero_plane

    for d in range(2):
        @pl.when(y == 3 * d)
        def _():
            ysg[d, 0] = jnp.zeros((2, 8, 128), F32)
            for par in range(2):
                yct[par, d, 0] = jnp.zeros((8, 128), F32)

    zz = (z + 8 * c) % 16
    home = zz < 8

    def landing(a):
        return ct.at[0, pl.ds(1, 8)] if a == 0 else tv.at[a - 1]

    def landing_two(a):
        return ct.at[0, pl.ds(1 + 2 * y, 2)] if a == 0 else tv.at[a - 1, pl.ds(2 * y, 2)]

    def in_copy(a, d):
        yt = (y + d) % 4
        rows = pl.ds(pl.multiple_of(32 * yt, 32), 32)
        return remote(inp.at[a, :, rows], landing_two(a), in_s.at[a, d], in_r.at[a], dev(x, yt, z, c))

    def in_local(a):
        rows = pl.ds(pl.multiple_of(32 * y, 32), 32)
        return pltpu.make_async_copy(inp.at[a, :, rows], landing_two(a), in_r.at[a])

    @pl.when(home)
    def _():
        for a in range(5):
            for d in range(1, 4):
                in_copy(a, d).start()
            in_local(a).start()

    up = jnp.where((zz >= 7) & (zz <= 10), 1, 0)
    down = jnp.where((zz == 0) | (zz >= 13), 1, 0)
    zt = (z + up + 15 * down) % 16

    def relay(a):
        return remote(landing(a), landing(a), rel_s.at[a], in_r.at[a], dev(x, y, zt, c))

    for a in range(5):
        arrived(landing(a), in_r.at[a])

        @pl.when(up + down > 0)
        def _():
            relay(a).start()

    def swap_copies(which, j):
        up4 = (j + zh + 1) % 2
        zt4 = (z + 4 * up4 + 12 * (1 - up4)) % 16
        copies = []
        for yt in range(4):
            where = dev(x, yt, zt4, c)
            if which == 2:
                copies.append(remote(meta.at[j], mbuf.at[zh * 4 + y], sw_s.at[2, j, yt], sw_r.at[2], where))
            else:
                src = (pot, adj)[which].at[j, :, pl.ds(32 * yt, 32)]
                dst = (pf, af)[which].at[0, 1 + zh, pl.ds(1 + 2 * y, 2)]
                copies.append(remote(src, dst, sw_s.at[which, j, yt], sw_r.at[which], where))
        return copies

    for which in (2, 0, 1):
        for j in range(2):
            for copy in swap_copies(which, j):
                copy.start()

    @pl.when(up + down > 0)
    def _():
        for a in range(5):
            relay(a).wait_send()

    def t_copies(par):
        return [
            remote(ct.at[par, 8], ct.at[par, 10 * x_last * c], t_s.at[par, 0], t_r.at[par, 0],
                   dev(xn, y, z, (c + x_last) % 2)),
            remote(ct.at[par, 1], ct.at[par, 9 + 2 * x_first * (1 - c)], t_s.at[par, 1], t_r.at[par, 1],
                   dev(xp, y, z, (c + x_first) % 2)),
            remote(yst.at[par, 0], yct.at[par, 0, y_last], t_s.at[par, 2], t_r.at[par, 2], dev(x, yn, z, c)),
            remote(yst.at[par, 1], yct.at[par, 1, y_first], t_s.at[par, 3], t_r.at[par, 3], dev(x, yp, z, c)),
        ]

    row = iota((32, 128), 0)
    lane = iota((32, 128), 1)

    def shift_y(v, low, high):
        below = jnp.where(row == 0, low, pltpu.roll(v, 1, 0))
        above = jnp.where(row == 31, high, pltpu.roll(v, 31, 0))
        return below, above

    def t_rows(par, p, v):
        yst[par, 0, pl.ds(p, 1), :] = v[31:32]
        yst[par, 1, pl.ds(p, 1), :] = v[0:1]

    def first_rows(p, carry):
        t_rows(0, p, ct[0, p + 1])
        return carry

    lax.fori_loop(0, 8, first_rows, 0)
    for copy in t_copies(0):
        copy.start()

    def t_step(s, carry):
        par = s % 2
        new = 1 - par
        for copy in t_copies(par):
            copy.wait()

        def plane(p, inner):
            v = ct[par, p + 1]
            xlow = ct[par, p]
            xhigh = ct[par, p + 2]
            ylow, yhigh = shift_y(v, yct[par, 0, 0, pl.ds(p, 1), :], yct[par, 1, 0, pl.ds(p, 1), :])
            zlow = jnp.where(lane == 0, 0.0, pltpu.roll(v, 1, 1))
            zhigh = jnp.where(lane == 127, 0.0, pltpu.roll(v, 127, 1))
            change = jnp.zeros((32, 128), F32)
            for d, (low, high) in enumerate(((xlow, xhigh), (ylow, yhigh), (zlow, zhigh))):
                speed = tv[d, p]
                change = change + jnp.maximum(speed, 0.0) * (v - low) + jnp.minimum(speed, 0.0) * (high - v)
            v = v - change
            ct[new, p + 1] = v
            t_rows(new, p, v)
            return inner

        lax.fori_loop(0, 8, plane, 0)

        @pl.when(s < STEPS - 1)
        def _():
            for copy in t_copies(new):
                copy.start()

        return carry

    lax.fori_loop(0, STEPS, t_step, 0)

    def conduct(p, carry):
        v = jnp.exp(1.8 * jnp.log(tv[3, p])) * (0.5 + ct[0, p + 1])
        sg[1 + c, p + 1] = v
        yss[0, pl.ds(p, 1), :] = v[31:32]
        yss[1, pl.ds(p, 1), :] = v[0:1]
        return carry

    lax.fori_loop(0, 8, conduct, 0)

    def sg_copies():
        copies = []
        for cc in range(2):
            copies += [
                remote(sg.at[1 + c, 8], sg.at[1 + c + x_last, 0], sg_s.at[0, cc], sg_r.at[0, c], dev(xn, y, z, cc)),
                remote(sg.at[1 + c, 1], sg.at[1 + c - x_first, 9], sg_s.at[1, cc], sg_r.at[1, c], dev(xp, y, z, cc)),
                remote(yss.at[0], ysg.at[0, y_last, c], sg_s.at[2, cc], sg_r.at[2, c], dev(x, yn, z, cc)),
                remote(yss.at[1], ysg.at[1, y_first, c], sg_s.at[3, cc], sg_r.at[3, c], dev(x, yp, z, cc)),
            ]
        return copies

    tile_copy = remote(
        sg.at[1 + c, pl.ds(1, 8)], sg.at[1 + c, pl.ds(1, 8)], tile_s, tile_r, dev(x, y, z, 1 - c)
    )
    tile_copy.start()
    for copy in sg_copies():
        copy.start()

    arrived(mbuf, sw_r.at[2])

    def tables(k, carry):
        q = iota((64, 128), 0)
        target = ((q // 32) * 128 + q % 32 + 32 * y).astype(F32)
        rt[k] = jnp.where(target == mbuf[k, 0:1, :], 1.0, 0.0)
        lt[k] = jnp.where(iota((128, 128), 0).astype(F32) == mbuf[k, 1:2, :], 1.0, 0.0)
        return carry

    lax.fori_loop(0, 8, tables, 0)
    jj = iota((128, 128), 0)
    mm = iota((128, 128), 1)
    spread = jnp.where((jj % 16 == mm % 16) & (mm < 64), 0.25, 0.0)
    own = jnp.where(iota((8, 128), 1) // 16 == iota((8, 128), 0), 1.0, 0.0)
    r0 = mbuf[0, 2:3, :]
    r1 = mbuf[0, 3:4, :]
    observed = mbuf[0, 4:5, :]
    ja = mbuf[0, 5:6, :]
    jb = mbuf[0, 6:7, :]

    tile_copy.wait()
    for copy in sg_copies():
        copy.wait_send()
    for d in range(4):
        for cc in range(2):
            if d < 2:
                arrived(sg.at[1, 0], sg_r.at[d, cc])
            else:
                arrived(yss.at[0], sg_r.at[d, cc])

    def faces_of(h, p):
        s = sg[1 + h, p + 1]
        low = ysg[0, 0, h, pl.ds(p, 1), :]
        high = ysg[1, 0, h, pl.ds(p, 1), :]
        _, syp = shift_y(s, low, high)
        szp = jnp.where(lane == 127, 0.0, pltpu.roll(s, 127, 1))
        ux = harmonic(s, sg[1 + h, p + 2])
        uy = harmonic(s, syp)
        uz = harmonic(s, szp)
        return s, low, ux, uy, uz

    def coefficients(h):
        def plane(p, lx):
            s, low, ux, uy, uz = faces_of(h, p)
            ly = jnp.where(row == 0, harmonic(low, s[0:1]), pltpu.roll(uy, 1, 0))
            lz = pltpu.roll(uz, 1, 1)
            r = 0.8 / (ux + lx + uy + ly + uz + lz)
            rdiag[h, p] = r
            for k, face in enumerate((ux, lx, uy, ly, uz, lz)):
                coef[k, h, p] = face * r
            return ux

        lax.fori_loop(0, 8, plane, harmonic(sg[1 + h, 0], sg[1 + h, 1]))

    for h in range(2):
        coefficients(h)

    def inject(current):
        vals = dot(jnp.broadcast_to(current, (8, 128)) * own, spread)
        for k in range(8):
            h, pair = k // 4, 2 * (k % 4)
            block = dot_t(rt[k], lt[k] * vals[k : k + 1, :])
            bsrc[h, pair] = block[0:32] * rdiag[h, pair]
            bsrc[h, pair + 1] = block[32:64] * rdiag[h, pair + 1]

    def field(f, yf, ysend, s_sem, r_sem):
        def copies(par):
            return [
                remote(f.at[par, pl.ds(1, 2), 8], f.at[par, pl.ds(1 + x_last, 2), 0],
                       s_sem.at[par, 0], r_sem.at[par, 0], dev(xn, y, z, c)),
                remote(f.at[par, pl.ds(1, 2), 1], f.at[par, pl.ds(1 - x_first, 2), 9],
                       s_sem.at[par, 1], r_sem.at[par, 1], dev(xp, y, z, c)),
                remote(ysend.at[par, 0], yf.at[par, 0], s_sem.at[par, 2], r_sem.at[par, 2], dev(x, yn, z, c)),
                remote(ysend.at[par, 1], yf.at[par, 1], s_sem.at[par, 3], r_sem.at[par, 3], dev(x, yp, z, c)),
            ]

        def edge_rows(par, h, p, v):
            ysend[par, 0, h, pl.ds(p, 1), :] = v[31:32]
            ysend[par, 1, h, pl.ds(p, 1), :] = v[0:1]

        def begin():
            for h in range(2):
                def plane(p, carry):
                    edge_rows(0, h, p, f[0, 1 + h, p + 1])
                    return carry

                lax.fori_loop(0, 8, plane, 0)
            for copy in copies(0):
                copy.start()

        def sweep(s, carry):
            par = s % 2
            new = 1 - par
            for copy in copies(par):
                copy.wait()
            for h in range(2):
                def plane(p, inner):
                    v = f[par, 1 + h, p + 1]
                    ylow, yhigh = shift_y(v, yf[par, 0, h, pl.ds(p, 1), :], yf[par, 1, h, pl.ds(p, 1), :])
                    out = coef[0, h, p] * f[par, 1 + h, p + 2] + coef[1, h, p] * f[par, 1 + h, p]
                    out = out + (coef[2, h, p] * yhigh + coef[3, h, p] * ylow)
                    out = out + (coef[4, h, p] * pltpu.roll(v, 127, 1) + coef[5, h, p] * pltpu.roll(v, 1, 1))
                    out = (0.2 * v + bsrc[h, p]) + out
                    f[new, 1 + h, p + 1] = out
                    edge_rows(new, h, p, out)
                    return inner

                lax.fori_loop(0, 8, plane, 0)
            for copy in copies(new):
                copy.start()
            return carry

        def sweeps():
            lax.fori_loop(0, RELAX_SWEEPS, sweep, 0)

        def end():
            for copy in copies(0):
                copy.wait()

        return begin, sweeps, end

    def electrode_ids(x_):
        j = iota((128, 128), 0)
        return ((j // 64) * 256 + x_ * 64 + j % 64).astype(F32)

    own_lane = iota((1, 128), 1)
    own_ids = ((own_lane // 64) * 256 + x * 64 + own_lane % 64).astype(F32)
    inject(4.0 * (jnp.where(own_ids == ja, 1.0, 0.0) - jnp.where(own_ids == jb, 1.0, 0.0)))

    p_begin, p_sweeps, p_end = field(pf, ypf, ypsend, p_s, p_r)
    a_begin, a_sweeps, a_end = field(af, yaf, yasend, a_s, a_r)
    arrived(pf.at[0, pl.ds(1, 2), pl.ds(1, 8)], sw_r.at[0])
    p_begin()
    p_sweeps()

    for k in range(8):
        h, pair = k // 4, 2 * (k % 4)
        block = pf[0, 1 + h, pl.ds(1 + pair, 2)].reshape(64, 128)
        vb[k : k + 1, :] = jnp.sum(rt[k] * dot(block, lt[k]), axis=0, keepdims=True)
    part = jnp.sum(dot_t(vb[...], spread) * own, axis=0, keepdims=True)
    vsend[...] = jnp.broadcast_to(part, (8, 128))

    def v_copy(k):
        xt = (x + k // 4) % 4
        yt = (y + k % 4) % 4
        return remote(vsend, vall.at[x * 4 + y], v_s.at[k], v_r, dev(xt, yt, z, c))

    for k in range(1, 16):
        v_copy(k).start()
    pltpu.make_async_copy(vsend, vall.at[x * 4 + y], v_r).start()
    arrived(af.at[0, pl.ds(1, 2), pl.ds(1, 8)], sw_r.at[1])
    a_begin()
    arrived(vall, v_r)

    def selector(x_):
        ids = electrode_ids(x_)
        return jnp.where(ids == r0, 1.0, 0.0) - jnp.where(ids == r1, 1.0, 0.0)

    readings = jnp.zeros((8, 128), F32)
    for k in range(4):
        volts = vall[4 * k] + vall[4 * k + 1] + vall[4 * k + 2] + vall[4 * k + 3]
        readings = readings + dot(volts, selector(k))
    rsend[...] = readings
    survey = (1 + zh + zl // 4) % 2

    def read_copies():
        return [
            remote(rsend, rdin.at[survey], rd_s.at[half], rd_r, dev(x, y, half * 8 + (zl + 4) % 8, c))
            for half in range(2)
        ]

    for copy in read_copies():
        copy.start()
    inject(dot_t(readings - observed, selector(x))[0:1])
    a_sweeps()
    p_end()
    a_end()

    for h in range(2):
        def terms(p, carry):
            _, _, ux, uy, uz = faces_of(h, p)
            pv = pf[0, 1 + h, p + 1]
            av = af[0, 1 + h, p + 1]
            _, py = shift_y(pv, pv[0:1], ypf[0, 1, h, pl.ds(p, 1), :])
            _, ay = shift_y(av, av[0:1], yaf[0, 1, h, pl.ds(p, 1), :])
            out = ux * (pf[0, 1 + h, p + 2] - pv) * (af[0, 1 + h, p + 2] - av)
            out = out + uy * (py - pv) * (ay - av)
            out = out + uz * (pltpu.roll(pv, 127, 1) - pv) * (pltpu.roll(av, 127, 1) - av)
            gbuf[h, p] = -out
            return carry

        lax.fori_loop(0, 8, terms, 0)

    other = remote(gbuf.at[1 - c], grx, gx_s, gx_r, dev(x, y, z, 1 - c))
    other.start()
    other.wait()

    def pair_sum(p, carry):
        gsum[p] = gbuf[c, p] + grx[p]
        return carry

    lax.fori_loop(0, 8, pair_sum, 0)

    def rs_copy(k, local):
        p, rh = k // 2, k % 2
        src = gsum.at[p, pl.ds(16 * rh, 16)]
        dst = rsbuf.at[z]
        if local:
            return pltpu.make_async_copy(src, dst, rs_r)
        return remote(src, dst, rs_s.at[k], rs_r, dev(x, y, 8 * c + p, rh))

    def rs_self(k):
        return (z == 8 * c + k // 2) & (c == k % 2)

    for k in range(16):
        @pl.when(jnp.logical_not(rs_self(k)))
        def _():
            rs_copy(k, False).start()

        @pl.when(rs_self(k))
        def _():
            rs_copy(k, True).start()

    arrived(rsbuf, rs_r)
    total = rsbuf[0]
    for k in range(1, 16):
        total = total + rsbuf[k]
    osum[...] = total

    def ag_copy(k, local):
        dst = grad.at[zl % 2, pl.ds(pl.multiple_of(32 * y + 16 * c, 16), 16)]
        if local:
            return pltpu.make_async_copy(osum, dst, ag_r)
        return remote(osum, dst, ag_s.at[k], ag_r, dev(x, zl // 2, 8 * zh + k // 2, k % 2))

    def ag_self(k):
        return (y == zl // 2) & (zl == k // 2) & (c == k % 2)

    for k in range(16):
        @pl.when(jnp.logical_not(ag_self(k)))
        def _():
            ag_copy(k, False).start()

        @pl.when(ag_self(k))
        def _():
            ag_copy(k, True).start()

    arrived(rdin, rd_r)
    read[0:1, :] = rdin[0, 0:1, :]
    read[1:2, :] = rdin[1, 0:1, :]
    arrived(grad, ag_r)

    @pl.when(home)
    def _():
        for a in range(5):
            for d in range(1, 4):
                in_copy(a, d).wait_send()

    for which in range(3):
        for j in range(2):
            for copy in swap_copies(which, j):
                copy.wait_send()
    for k in range(1, 16):
        v_copy(k).wait_send()
    for copy in read_copies():
        copy.wait_send()
    for k in range(16):
        @pl.when(jnp.logical_not(rs_self(k)))
        def _():
            rs_copy(k, False).wait_send()

        @pl.when(jnp.logical_not(ag_self(k)))
        def _():
            ag_copy(k, False).wait_send()


def on_device(
    concentration, velocity, porosity, contacts, sources, receivers, observed, potential_init, adjoint_init
):
    inp = jnp.concatenate([concentration[None], velocity.astype(F32), porosity[None]], axis=0)
    cells = contacts.T.reshape(1, 64)
    pad = jnp.full((1, 64), -1, jnp.int32)
    where = jnp.concatenate([cells // 128, pad], axis=1).astype(F32)
    lanes = jnp.concatenate([cells % 128, pad], axis=1).astype(F32)
    gap = jnp.full((2, 64), -1.0, F32)
    meta = jnp.stack(
        [
            jnp.broadcast_to(where, (2, 128)),
            jnp.broadcast_to(lanes, (2, 128)),
            jnp.concatenate([receivers[:, :, 0].astype(F32), gap], axis=1),
            jnp.concatenate([receivers[:, :, 1].astype(F32), gap], axis=1),
            jnp.concatenate([observed, jnp.zeros((2, 64), F32)], axis=1),
            jnp.broadcast_to(sources[:, 0:1].astype(F32), (2, 128)),
            jnp.broadcast_to(sources[:, 1:2].astype(F32), (2, 128)),
            jnp.zeros((2, 128), F32),
        ],
        axis=1,
    )
    V = pltpu.VMEM
    D = pltpu.SemaphoreType.DMA
    scratch = [
        V((2, 12, 32, 128), F32), V((2, 2, 2, 8, 128), F32), V((2, 2, 8, 128), F32), V((4, 8, 32, 128), F32),
        V((4, 10, 32, 128), F32), V((2, 2, 2, 8, 128), F32), V((2, 8, 128), F32),
        V((6, 2, 8, 32, 128), F32), V((2, 8, 32, 128), F32), V((2, 8, 32, 128), F32),
        V((2, 4, 10, 32, 128), F32), V((2, 2, 2, 8, 128), F32), V((2, 2, 2, 8, 128), F32),
        V((2, 4, 10, 32, 128), F32), V((2, 2, 2, 8, 128), F32), V((2, 2, 2, 8, 128), F32),
        V((8, 8, 128), F32), V((8, 64, 128), F32), V((8, 128, 128), F32), V((8, 128), F32), V((8, 128), F32),
        V((16, 8, 128), F32), V((8, 128), F32), V((2, 8, 128), F32),
        V((2, 8, 32, 128), F32), V((8, 32, 128), F32), V((8, 32, 128), F32), V((16, 16, 128), F32), V((16, 128), F32),
        D((5, 4)), D((5,)), D((5,)), D((2, 4)), D((2, 4)), D((3, 2, 4)), D((3,)), D((4, 2)), D((4, 2)), D, D,
        D((2, 4)), D((2, 4)), D((2, 4)), D((2, 4)), D((16,)), D, D((2,)), D, D, D, D((16,)), D, D((16,)), D,
    ]
    gradient, readings = pl.pallas_call(
        kernel,
        out_shape=(jax.ShapeDtypeStruct((2, 128, 128), F32), jax.ShapeDtypeStruct((2, 128), F32)),
        in_specs=[pl.BlockSpec(memory_space=pl.ANY)] * 4,
        out_specs=(pl.BlockSpec(memory_space=pltpu.VMEM), pl.BlockSpec(memory_space=pltpu.VMEM)),
        scratch_shapes=scratch,
        compiler_params=pltpu.CompilerParams(has_side_effects=True),
        name="survey_gradient",
    )(inp, potential_init, adjoint_init, meta)
    return gradient, readings[:, :64]


def solution(mesh):
    return jax.shard_map(
        on_device,
        mesh=mesh,
        in_specs=(
            P("space", None, None),
            P(None, "space", None, None),
            P("space", None, None),
            P("space", None),
            P("tm", None),
            P("tm", None, None),
            P("tm", None),
            P("tm", "space", None, None),
            P("tm", "space", None, None),
        ),
        out_specs=(P("space", None, None), P("tm", None)),
        check_vma=False,
    )
```

```python
import jax
import jax.numpy as jnp
from jax import lax
from jax.experimental import pallas as pl
from jax.experimental.pallas import tpu as pltpu
from jax.sharding import PartitionSpec as P

STEPS = 8
RELAX_SWEEPS = 6
MESH = pl.DeviceIdType.MESH
HIGH = lax.Precision.HIGHEST
F32 = jnp.float32


def harmonic(first, second):
    return 2.0 * (first * second) / (first + second)


def iota(shape, dim):
    return lax.broadcasted_iota(jnp.int32, shape, dim)


def dot(a, b):
    return lax.dot_general(a, b, (((1,), (0,)), ((), ())), precision=HIGH, preferred_element_type=F32)


def dot_t(a, b):
    return lax.dot_general(a, b, (((1,), (1,)), ((), ())), precision=HIGH, preferred_element_type=F32)


def kernel(
    inp, pot, adj, meta, grad, read,
    ct, yct, yst, tv, sg, ysg, yss, coef, rdiag, bsrc,
    pf, ypf, ypsend, af, yaf, yasend,
    mbuf, rt, lt, vb, vsend, vall, rsend, rdin,
    gbuf, grx, gsum, rsbuf, osum,
    in_s, in_r, rel_s, t_s, t_r, sw_s, sw_r, sg_s, sg_r, tile_s, tile_r,
    p_s, p_r, a_s, a_r, v_s, v_r, rd_s, rd_r, gx_s, gx_r, rs_s, rs_r, ag_s, ag_r,
):
    space = lax.axis_index("space")
    tm = lax.axis_index("tm")
    zh = space // 16
    x = (space // 4) % 4
    y = space % 4
    zl = tm // 2
    c = tm % 2
    z = zh * 8 + zl

    def dev(x_, y_, z_, c_):
        return {"space": (z_ // 8) * 16 + x_ * 4 + y_, "tm": (z_ % 8) * 2 + c_}

    def remote(src, dst, s, r, where):
        return pltpu.make_async_remote_copy(
            src_ref=src, dst_ref=dst, send_sem=s, recv_sem=r, device_id=where, device_id_type=MESH
        )

    def arrived(ref, sem):
        pltpu.make_async_copy(ref, ref, sem).wait()

    def start_y(copies):
        @pl.when(y < 3)
        def _():
            copies[0].start()

        @pl.when(y > 0)
        def _():
            copies[1].start()

    def wait_y(copies):
        @pl.when(y < 3)
        def _():
            copies[0].wait_send()
            copies[1].wait_recv()

        @pl.when(y > 0)
        def _():
            copies[1].wait_send()
            copies[0].wait_recv()

    xn = (x + 1) % 4
    xp = (x + 3) % 4
    yn = (y + 1) % 4
    yp = (y + 3) % 4
    x_last = (x + 1) // 4
    x_first = (3 - x) // 3

    zero_plane = jnp.zeros((32, 128), F32)

    @pl.when((x == 0) & (c == 0))
    def _():
        for par in range(2):
            ct[par, 0] = zero_plane

    @pl.when((x == 3) & (c == 1))
    def _():
        for par in range(2):
            ct[par, 9] = zero_plane

    @pl.when(x == 0)
    def _():
        sg[1, 0] = zero_plane
        for f in (pf, af):
            for par in range(2):
                f[par, 1, 0] = zero_plane

    @pl.when(x == 3)
    def _():
        sg[2, 9] = zero_plane
        for f in (pf, af):
            for par in range(2):
                f[par, 2, 9] = zero_plane

    for d in range(2):
        @pl.when(y == 3 * d)
        def _():
            ysg[d, 0] = jnp.zeros((2, 8, 128), F32)
            for yf in (ypf, yaf):
                for par in range(2):
                    yf[par, d] = jnp.zeros((2, 8, 128), F32)
            for par in range(2):
                yct[par, d, 0] = jnp.zeros((8, 128), F32)

    barrier = pltpu.get_barrier_semaphore()

    def greet(where):
        pl.semaphore_signal(barrier, inc=1, device_id=where, device_id_type=MESH)

    def greet_half(k, carry):
        greet(dev(x, (y + k // 16) % 4, 8 * zh + (zl + (k // 2) % 8) % 8, (c + k % 2) % 2))
        return carry

    def greet_column(k, carry):
        greet(dev(x, y, 8 * (1 - zh) + k // 2, k % 2))
        return carry

    def greet_far(k, carry):
        greet(dev(x, (y + k) % 4, (z + 4 * (zl // 4) + 12 * (1 - zl // 4)) % 16, c))
        return carry

    def greet_plane(k, carry):
        greet(dev((x + 1 + k // 8) % 4, (k // 2) % 4, z, k % 2))
        return carry

    lax.fori_loop(0, 16, greet_column, 0)
    lax.fori_loop(1, 4, greet_far, 0)
    lax.fori_loop(1, 64, greet_half, 0)
    lax.fori_loop(0, 24, greet_plane, 0)
    pl.semaphore_wait(barrier, 16 + 3 + 63 + 24)

    zz = (z + 8 * c) % 16
    home = zz < 8

    def landing(a):
        return ct.at[0, pl.ds(1, 8)] if a == 0 else tv.at[a - 1]

    def landing_two(a):
        return ct.at[0, pl.ds(1 + 2 * y, 2)] if a == 0 else tv.at[a - 1, pl.ds(2 * y, 2)]

    def in_copy(a, d):
        yt = (y + d) % 4
        rows = pl.ds(pl.multiple_of(32 * yt, 32), 32)
        return remote(inp.at[a, :, rows], landing_two(a), in_s.at[a, d], in_r.at[a], dev(x, yt, z, c))

    def in_local(a):
        rows = pl.ds(pl.multiple_of(32 * y, 32), 32)
        return pltpu.make_async_copy(inp.at[a, :, rows], landing_two(a), in_r.at[a])

    @pl.when(home)
    def _():
        for a in range(5):
            for d in range(1, 4):
                in_copy(a, d).start()
            in_local(a).start()

    up = jnp.where((zz >= 7) & (zz <= 10), 1, 0)
    down = jnp.where((zz == 0) | (zz >= 13), 1, 0)
    zt = (z + up + 15 * down) % 16

    def relay(a):
        return remote(landing(a), landing(a), rel_s.at[a], in_r.at[a], dev(x, y, zt, c))

    for a in range(5):
        arrived(landing(a), in_r.at[a])

        @pl.when(up + down > 0)
        def _():
            relay(a).start()

    def swap_copy(which, j, d):
        up4 = (j + zh + 1) % 2
        zt4 = (z + 4 * up4 + 12 * (1 - up4)) % 16
        yt = (y + d) % 4
        where = dev(x, yt, zt4, c)
        if which == 2:
            return remote(meta.at[j], mbuf.at[zh * 4 + y], sw_s.at[2, j, d], sw_r.at[2], where)
        src = (pot, adj)[which].at[j, :, pl.ds(pl.multiple_of(32 * yt, 32), 32)]
        dst = (pf, af)[which].at[0, 1 + zh, pl.ds(1 + 2 * y, 2)]
        return remote(src, dst, sw_s.at[which, j, d], sw_r.at[which], where)

    def swap_copies(which, j):
        return [swap_copy(which, j, d) for d in range(4)]

    for j in range(2):
        for copy in swap_copies(2, j):
            copy.start()

    @pl.when(up + down > 0)
    def _():
        for a in range(5):
            relay(a).wait_send()

    def t_x(par):
        return [
            remote(ct.at[par, 8], ct.at[par, 10 * x_last * c], t_s.at[par, 0], t_r.at[par, 0],
                   dev(xn, y, z, (c + x_last) % 2)),
            remote(ct.at[par, 1], ct.at[par, 9 + 2 * x_first * (1 - c)], t_s.at[par, 1], t_r.at[par, 1],
                   dev(xp, y, z, (c + x_first) % 2)),
        ]

    def t_y(par):
        return [
            remote(yst.at[par, 0], yct.at[par, 0, 0], t_s.at[par, 2], t_r.at[par, 2], dev(x, yn, z, c)),
            remote(yst.at[par, 1], yct.at[par, 1, 0], t_s.at[par, 3], t_r.at[par, 3], dev(x, yp, z, c)),
        ]

    row = iota((32, 128), 0)
    lane = iota((32, 128), 1)

    def shift_y(v, low, high):
        below = jnp.where(row == 0, low, pltpu.roll(v, 1, 0))
        above = jnp.where(row == 31, high, pltpu.roll(v, 31, 0))
        return below, above

    def t_rows(par, p, v):
        yst[par, 0, p : p + 1, :] = v[31:32]
        yst[par, 1, p : p + 1, :] = v[0:1]

    for copy in t_x(0):
        copy.start()
    for p in range(8):
        t_rows(0, p, ct[0, p + 1])
    start_y(t_y(0))

    def t_step(par, last):
        new = 1 - par

        def plane(p):
            v = ct[par, p + 1]
            xlow = ct[par, p]
            xhigh = ct[par, p + 2]
            ylow, yhigh = shift_y(v, yct[par, 0, 0, p : p + 1, :], yct[par, 1, 0, p : p + 1, :])
            zlow = jnp.where(lane == 0, 0.0, pltpu.roll(v, 1, 1))
            zhigh = jnp.where(lane == 127, 0.0, pltpu.roll(v, 127, 1))
            change = None
            for d, (low, high) in enumerate(((xlow, xhigh), (ylow, yhigh), (zlow, zhigh))):
                speed = tv[d, p]
                term = jnp.maximum(speed, 0.0) * (v - low) + jnp.minimum(speed, 0.0) * (high - v)
                change = term if change is None else change + term
            v = v - change
            ct[new, p + 1] = v
            t_rows(new, p, v)

        wait_y(t_y(par))
        for copy in t_x(par):
            copy.wait()
        plane(0)
        plane(7)

        @pl.when(jnp.logical_not(last))
        def _():
            for copy in t_x(new):
                copy.start()

        for p in range(1, 7):
            plane(p)

        @pl.when(jnp.logical_not(last))
        def _():
            start_y(t_y(new))

    def t_two(s, carry):
        t_step(0, s < 0)

        @pl.when(s < 2)
        def _():
            swap_copy(0, s % 2, 0).start()
            swap_copy(0, s % 2, 1).start()

        @pl.when(s >= 2)
        def _():
            swap_copy(1, s % 2, 0).start()
            swap_copy(1, s % 2, 1).start()

        t_step(1, s == STEPS // 2 - 1)

        @pl.when(s < 2)
        def _():
            swap_copy(0, s % 2, 2).start()
            swap_copy(0, s % 2, 3).start()

        @pl.when(s >= 2)
        def _():
            swap_copy(1, s % 2, 2).start()
            swap_copy(1, s % 2, 3).start()

        return carry

    lax.fori_loop(0, STEPS // 2, t_two, 0)

    for p in range(8):
        v = jnp.exp(1.8 * jnp.log(tv[3, p])) * (0.5 + ct[0, p + 1])
        sg[1 + c, p + 1] = v
        yss[0, p : p + 1, :] = v[31:32]
        yss[1, p : p + 1, :] = v[0:1]

    def sg_x(cc):
        return [
            remote(sg.at[1 + c, 8], sg.at[1 + c + x_last, 0], sg_s.at[0, cc], sg_r.at[0, c], dev(xn, y, z, cc)),
            remote(sg.at[1 + c, 1], sg.at[1 + c - x_first, 9], sg_s.at[1, cc], sg_r.at[1, c], dev(xp, y, z, cc)),
        ]

    def sg_y(cc):
        return [
            remote(yss.at[0], ysg.at[0, 0, c], sg_s.at[2, cc], sg_r.at[2, c], dev(x, yn, z, cc)),
            remote(yss.at[1], ysg.at[1, 0, c], sg_s.at[3, cc], sg_r.at[3, c], dev(x, yp, z, cc)),
        ]

    tile_copy = remote(
        sg.at[1 + c, pl.ds(1, 8)], sg.at[1 + c, pl.ds(1, 8)], tile_s, tile_r, dev(x, y, z, 1 - c)
    )
    tile_copy.start()
    for cc in range(2):
        start_y(sg_y(cc))
        for copy in sg_x(cc):
            copy.start()

    arrived(mbuf, sw_r.at[2])

    def tables(k, carry):
        q = iota((64, 128), 0)
        target = ((q // 32) * 128 + q % 32 + 32 * y).astype(F32)
        rt[k] = jnp.where(target == mbuf[k, 0:1, :], 1.0, 0.0)
        lt[k] = jnp.where(iota((128, 128), 0).astype(F32) == mbuf[k, 1:2, :], 1.0, 0.0)
        return carry

    lax.fori_loop(0, 8, tables, 0)
    jj = iota((128, 128), 0)
    mm = iota((128, 128), 1)
    spread = jnp.where((jj % 16 == mm % 16) & (mm < 64), 0.25, 0.0)
    own = jnp.where(iota((8, 128), 1) // 16 == iota((8, 128), 0), 1.0, 0.0)
    r0 = mbuf[0, 2:3, :]
    r1 = mbuf[0, 3:4, :]
    observed = mbuf[0, 4:5, :]
    ja = mbuf[0, 5:6, :]
    jb = mbuf[0, 6:7, :]

    tile_copy.wait()
    for cc in range(2):
        for d, copy in enumerate(sg_x(cc)):
            copy.wait_send()
            arrived(sg.at[1, 0], sg_r.at[d, cc])

        @pl.when(y < 3)
        def _():
            sg_y(cc)[0].wait_send()
            arrived(yss.at[0], sg_r.at[3, cc])

        @pl.when(y > 0)
        def _():
            sg_y(cc)[1].wait_send()
            arrived(yss.at[0], sg_r.at[2, cc])

    def faces_of(h, p):
        s = sg[1 + h, p + 1]
        low = ysg[0, 0, h, p : p + 1, :]
        high = ysg[1, 0, h, p : p + 1, :]
        _, syp = shift_y(s, low, high)
        szp = jnp.where(lane == 127, 0.0, pltpu.roll(s, 127, 1))
        ux = harmonic(s, sg[1 + h, p + 2])
        uy = harmonic(s, syp)
        uz = harmonic(s, szp)
        return s, low, ux, uy, uz

    for h in range(2):
        lx = harmonic(sg[1 + h, 0], sg[1 + h, 1])
        for p in range(8):
            s, low, ux, uy, uz = faces_of(h, p)
            ly = jnp.where(row == 0, harmonic(low, s[0:1]), pltpu.roll(uy, 1, 0))
            lz = pltpu.roll(uz, 1, 1)
            r = 0.8 / (ux + lx + uy + ly + uz + lz)
            rdiag[h, p] = r
            for k, face in enumerate((ux, lx, uy, ly, uz, lz)):
                coef[k, h, p] = face * r
            lx = ux

    def inject(current):
        vals = dot(jnp.broadcast_to(current, (8, 128)) * own, spread)
        for k in range(8):
            h, pair = k // 4, 2 * (k % 4)
            block = dot_t(rt[k], lt[k] * vals[k : k + 1, :])
            bsrc[h, pair] = block[0:32] * rdiag[h, pair]
            bsrc[h, pair + 1] = block[32:64] * rdiag[h, pair + 1]

    def field(f, yf, ysend, s_sem, r_sem):
        def x_copies(par):
            return [
                remote(f.at[par, pl.ds(1, 2), 8], f.at[par, pl.ds(1 + x_last, 2), 0],
                       s_sem.at[par, 0], r_sem.at[par, 0], dev(xn, y, z, c)),
                remote(f.at[par, pl.ds(1, 2), 1], f.at[par, pl.ds(1 - x_first, 2), 9],
                       s_sem.at[par, 1], r_sem.at[par, 1], dev(xp, y, z, c)),
            ]

        def y_copies(par):
            return [
                remote(ysend.at[par, 0], yf.at[par, 0], s_sem.at[par, 2], r_sem.at[par, 2], dev(x, yn, z, c)),
                remote(ysend.at[par, 1], yf.at[par, 1], s_sem.at[par, 3], r_sem.at[par, 3], dev(x, yp, z, c)),
            ]

        def edge_rows(par, h, p, v):
            ysend[par, 0, h, p : p + 1, :] = v[31:32]
            ysend[par, 1, h, p : p + 1, :] = v[0:1]

        def begin():
            for copy in x_copies(0):
                copy.start()
            for h in range(2):
                for p in range(8):
                    edge_rows(0, h, p, f[0, 1 + h, p + 1])
            start_y(y_copies(0))

        def end(par=0):
            wait_y(y_copies(par))
            for copy in x_copies(par):
                copy.wait()

        def sweep(par):
            new = 1 - par

            def plane(h, p):
                v = f[par, 1 + h, p + 1]
                ylow, yhigh = shift_y(v, yf[par, 0, h, p : p + 1, :], yf[par, 1, h, p : p + 1, :])
                out = coef[0, h, p] * f[par, 1 + h, p + 2] + coef[1, h, p] * f[par, 1 + h, p]
                out = out + (coef[2, h, p] * yhigh + coef[3, h, p] * ylow)
                out = out + (coef[4, h, p] * pltpu.roll(v, 127, 1) + coef[5, h, p] * pltpu.roll(v, 1, 1))
                out = (0.2 * v + bsrc[h, p]) + out
                f[new, 1 + h, p + 1] = out
                edge_rows(new, h, p, out)

            end(par)
            for p in (0, 7):
                for h in range(2):
                    plane(h, p)
            for copy in x_copies(new):
                copy.start()
            for h in range(2):
                for p in range(1, 7):
                    plane(h, p)
            start_y(y_copies(new))

        def two(s, carry):
            sweep(0)
            sweep(1)
            return carry

        def sweeps():
            lax.fori_loop(0, RELAX_SWEEPS // 2, two, 0)

        return begin, sweeps, end

    def electrode_ids(x_):
        j = iota((128, 128), 0)
        return ((j // 64) * 256 + x_ * 64 + j % 64).astype(F32)

    own_lane = iota((1, 128), 1)
    own_ids = ((own_lane // 64) * 256 + x * 64 + own_lane % 64).astype(F32)
    inject(4.0 * (jnp.where(own_ids == ja, 1.0, 0.0) - jnp.where(own_ids == jb, 1.0, 0.0)))

    p_begin, p_sweeps, p_end = field(pf, ypf, ypsend, p_s, p_r)
    a_begin, a_sweeps, a_end = field(af, yaf, yasend, a_s, a_r)
    arrived(pf.at[0, pl.ds(1, 2), pl.ds(1, 8)], sw_r.at[0])
    p_begin()
    p_sweeps()

    for k in range(8):
        h, pair = k // 4, 2 * (k % 4)
        block = pf[0, 1 + h, pl.ds(1 + pair, 2)].reshape(64, 128)
        vb[k : k + 1, :] = jnp.sum(rt[k] * dot(block, lt[k]), axis=0, keepdims=True)
    part = jnp.sum(dot_t(vb[...], spread) * own, axis=0, keepdims=True)
    vsend[...] = jnp.broadcast_to(part, (8, 128))

    def v_copy(k):
        xt = (x + k // 4) % 4
        yt = (y + k % 4) % 4
        return remote(vsend, vall.at[x * 4 + y], v_s.at[k], v_r, dev(xt, yt, z, c))

    for k in range(1, 16):
        v_copy(k).start()
    pltpu.make_async_copy(vsend, vall.at[x * 4 + y], v_r).start()
    arrived(af.at[0, pl.ds(1, 2), pl.ds(1, 8)], sw_r.at[1])
    a_begin()
    arrived(vall, v_r)

    def selector(x_):
        ids = electrode_ids(x_)
        return jnp.where(ids == r0, 1.0, 0.0) - jnp.where(ids == r1, 1.0, 0.0)

    readings = jnp.zeros((8, 128), F32)
    for k in range(4):
        volts = vall[4 * k] + vall[4 * k + 1] + vall[4 * k + 2] + vall[4 * k + 3]
        readings = readings + dot(volts, selector(k))
    rsend[...] = readings
    survey = (1 + zh + zl // 4) % 2

    def read_copies():
        return [
            remote(rsend, rdin.at[survey], rd_s.at[half], rd_r, dev(x, y, half * 8 + (zl + 4) % 8, c))
            for half in range(2)
        ]

    for copy in read_copies():
        copy.start()
    inject(dot_t(readings - observed, selector(x))[0:1])
    a_sweeps()
    p_end()
    a_end()

    for h in range(2):
        for p in range(8):
            _, _, ux, uy, uz = faces_of(h, p)
            pv = pf[0, 1 + h, p + 1]
            av = af[0, 1 + h, p + 1]
            _, py = shift_y(pv, pv[0:1], ypf[0, 1, h, p : p + 1, :])
            _, ay = shift_y(av, av[0:1], yaf[0, 1, h, p : p + 1, :])
            out = ux * (pf[0, 1 + h, p + 2] - pv) * (af[0, 1 + h, p + 2] - av)
            out = out + uy * (py - pv) * (ay - av)
            out = out + uz * (pltpu.roll(pv, 127, 1) - pv) * (pltpu.roll(av, 127, 1) - av)
            gbuf[h, p] = -out

    other = remote(gbuf.at[1 - c], grx, gx_s, gx_r, dev(x, y, z, 1 - c))
    other.start()
    other.wait()

    for p in range(8):
        gsum[p] = gbuf[c, p] + grx[p]

    def rs_copy(k, local):
        p, rh = k // 2, k % 2
        src = gsum.at[p, pl.ds(16 * rh, 16)]
        dst = rsbuf.at[z]
        if local:
            return pltpu.make_async_copy(src, dst, rs_r)
        return remote(src, dst, rs_s.at[k], rs_r, dev(x, y, 8 * c + p, rh))

    def rs_self(k):
        return (z == 8 * c + k // 2) & (c == k % 2)

    for k in range(16):
        @pl.when(jnp.logical_not(rs_self(k)))
        def _():
            rs_copy(k, False).start()

        @pl.when(rs_self(k))
        def _():
            rs_copy(k, True).start()

    arrived(rsbuf, rs_r)
    total = rsbuf[0]
    for k in range(1, 16):
        total = total + rsbuf[k]
    osum[...] = total

    def ag_copy(k, local):
        dst = grad.at[zl % 2, pl.ds(pl.multiple_of(32 * y + 16 * c, 16), 16)]
        if local:
            return pltpu.make_async_copy(osum, dst, ag_r)
        return remote(osum, dst, ag_s.at[k], ag_r, dev(x, zl // 2, 8 * zh + k // 2, k % 2))

    def ag_self(k):
        return (y == zl // 2) & (zl == k // 2) & (c == k % 2)

    for k in range(16):
        @pl.when(jnp.logical_not(ag_self(k)))
        def _():
            ag_copy(k, False).start()

        @pl.when(ag_self(k))
        def _():
            ag_copy(k, True).start()

    arrived(rdin, rd_r)
    read[0:1, :] = rdin[0, 0:1, :]
    read[1:2, :] = rdin[1, 0:1, :]
    arrived(grad, ag_r)

    @pl.when(home)
    def _():
        for a in range(5):
            for d in range(1, 4):
                in_copy(a, d).wait_send()

    for which in range(3):
        for j in range(2):
            for copy in swap_copies(which, j):
                copy.wait_send()
    for k in range(1, 16):
        v_copy(k).wait_send()
    for copy in read_copies():
        copy.wait_send()
    for k in range(16):
        @pl.when(jnp.logical_not(rs_self(k)))
        def _():
            rs_copy(k, False).wait_send()

        @pl.when(jnp.logical_not(ag_self(k)))
        def _():
            ag_copy(k, False).wait_send()


def on_device(
    concentration, velocity, porosity, contacts, sources, receivers, observed, potential_init, adjoint_init
):
    inp = jnp.concatenate([concentration[None], velocity.astype(F32), porosity[None]], axis=0)
    cells = contacts.T.reshape(1, 64)
    pad = jnp.full((1, 64), -1, jnp.int32)
    where = jnp.concatenate([cells // 128, pad], axis=1).astype(F32)
    lanes = jnp.concatenate([cells % 128, pad], axis=1).astype(F32)
    gap = jnp.full((2, 64), -1.0, F32)
    meta = jnp.stack(
        [
            jnp.broadcast_to(where, (2, 128)),
            jnp.broadcast_to(lanes, (2, 128)),
            jnp.concatenate([receivers[:, :, 0].astype(F32), gap], axis=1),
            jnp.concatenate([receivers[:, :, 1].astype(F32), gap], axis=1),
            jnp.concatenate([observed, jnp.zeros((2, 64), F32)], axis=1),
            jnp.broadcast_to(sources[:, 0:1].astype(F32), (2, 128)),
            jnp.broadcast_to(sources[:, 1:2].astype(F32), (2, 128)),
            jnp.zeros((2, 128), F32),
        ],
        axis=1,
    )
    V = pltpu.VMEM
    D = pltpu.SemaphoreType.DMA
    scratch = [
        V((2, 12, 32, 128), F32), V((2, 2, 2, 8, 128), F32), V((2, 2, 8, 128), F32), V((4, 8, 32, 128), F32),
        V((4, 10, 32, 128), F32), V((2, 2, 2, 8, 128), F32), V((2, 8, 128), F32),
        V((6, 2, 8, 32, 128), F32), V((2, 8, 32, 128), F32), V((2, 8, 32, 128), F32),
        V((2, 4, 10, 32, 128), F32), V((2, 2, 2, 8, 128), F32), V((2, 2, 2, 8, 128), F32),
        V((2, 4, 10, 32, 128), F32), V((2, 2, 2, 8, 128), F32), V((2, 2, 2, 8, 128), F32),
        V((8, 8, 128), F32), V((8, 64, 128), F32), V((8, 128, 128), F32), V((8, 128), F32), V((8, 128), F32),
        V((16, 8, 128), F32), V((8, 128), F32), V((2, 8, 128), F32),
        V((2, 8, 32, 128), F32), V((8, 32, 128), F32), V((8, 32, 128), F32), V((16, 16, 128), F32), V((16, 128), F32),
        D((5, 4)), D((5,)), D((5,)), D((2, 4)), D((2, 4)), D((3, 2, 4)), D((3,)), D((4, 2)), D((4, 2)), D, D,
        D((2, 4)), D((2, 4)), D((2, 4)), D((2, 4)), D((16,)), D, D((2,)), D, D, D, D((16,)), D, D((16,)), D,
    ]
    gradient, readings = pl.pallas_call(
        kernel,
        out_shape=(jax.ShapeDtypeStruct((2, 128, 128), F32), jax.ShapeDtypeStruct((2, 128), F32)),
        in_specs=[pl.BlockSpec(memory_space=pl.ANY)] * 4,
        out_specs=(pl.BlockSpec(memory_space=pltpu.VMEM), pl.BlockSpec(memory_space=pltpu.VMEM)),
        scratch_shapes=scratch,
        compiler_params=pltpu.CompilerParams(collective_id=0, has_side_effects=True),
        name="survey_gradient",
    )(inp, potential_init, adjoint_init, meta)
    return gradient, readings[:, :64]


def solution(mesh):
    return jax.shard_map(
        on_device,
        mesh=mesh,
        in_specs=(
            P("space", None, None),
            P(None, "space", None, None),
            P("space", None, None),
            P("space", None),
            P("tm", None),
            P("tm", None, None),
            P("tm", None),
            P("tm", "space", None, None),
            P("tm", "space", None, None),
        ),
        out_specs=(P("space", None, None), P("tm", None)),
        check_vma=False,
    )
```

```python
import jax
import jax.numpy as jnp
from jax import lax
from jax.experimental import pallas as pl
from jax.experimental.pallas import tpu as pltpu
from jax.sharding import PartitionSpec as P

STEPS = 8
RELAX_SWEEPS = 6
MESH = pl.DeviceIdType.MESH
F32 = jnp.float32
BF16 = jnp.bfloat16


def harmonic(first, second):
    return 2.0 * (first * second) / (first + second)


def iota(shape, dim):
    return lax.broadcasted_iota(jnp.int32, shape, dim)


def parts(a):
    high = a.astype(BF16)
    rest = a - high.astype(F32)
    middle = rest.astype(BF16)
    low = (rest - middle.astype(F32)).astype(BF16)
    return jnp.concatenate([high, middle, low], axis=0)


def total(product):
    rows = product.shape[0] // 3
    return product[:rows] + (product[rows : 2 * rows] + product[2 * rows :])


def dot(a, exact):
    dims = (((1,), (0,)), ((), ()))
    return total(lax.dot_general(parts(a), exact.astype(BF16), dims, preferred_element_type=F32))


def dot_t(a, exact):
    dims = (((1,), (1,)), ((), ()))
    return total(lax.dot_general(parts(a), exact.astype(BF16), dims, preferred_element_type=F32))


def kernel(
    conc, vel, poro, contacts, sources, receivers, observed, pot, adj, grad, read,
    ct, yct, yst, tv, sg, ysg, yss, coef, rdiag, bsrc,
    pf, ypf, ypsend, af, yaf, yasend,
    mbuf, rt, lt, vb, vsend, vall, rsend, rdin,
    gbuf, grx, gsum, rsbuf, osum, vbf, vf, cin, sin, rin, oin, msend,
    in_s, in_r, rel_s, t_s, t_r, sw_s, sw_r, sg_s, sg_r, tile_s, tile_r,
    p_s, p_r, a_s, a_r, v_s, v_r, rd_s, rd_r, gx_s, gx_r, rs_s, rs_r, ag_s, ag_r, fetch,
):
    space = lax.axis_index("space")
    tm = lax.axis_index("tm")
    zh = space // 16
    x = (space // 4) % 4
    y = space % 4
    zl = tm // 2
    c = tm % 2
    z = zh * 8 + zl

    def dev(x_, y_, z_, c_):
        return {"space": (z_ // 8) * 16 + x_ * 4 + y_, "tm": (z_ % 8) * 2 + c_}

    def remote(src, dst, s, r, where):
        return pltpu.make_async_remote_copy(
            src_ref=src, dst_ref=dst, send_sem=s, recv_sem=r, device_id=where, device_id_type=MESH
        )

    def arrived(ref, sem):
        pltpu.make_async_copy(ref, ref, sem).wait()

    def start_y(copies):
        @pl.when(y < 3)
        def _():
            copies[0].start()

        @pl.when(y > 0)
        def _():
            copies[1].start()

    def wait_y(copies):
        @pl.when(y < 3)
        def _():
            copies[0].wait_send()
            copies[1].wait_recv()

        @pl.when(y > 0)
        def _():
            copies[1].wait_send()
            copies[0].wait_recv()

    xn = (x + 1) % 4
    xp = (x + 3) % 4
    yn = (y + 1) % 4
    yp = (y + 3) % 4
    x_last = (x + 1) // 4
    x_first = (3 - x) // 3

    zero_plane = jnp.zeros((32, 128), F32)

    @pl.when((x == 0) & (c == 0))
    def _():
        for par in range(2):
            ct[par, 0] = zero_plane

    @pl.when((x == 3) & (c == 1))
    def _():
        for par in range(2):
            ct[par, 9] = zero_plane

    @pl.when(x == 0)
    def _():
        sg[1, 0] = zero_plane
        for f in (pf, af):
            for par in range(2):
                f[par, 1, 0] = zero_plane

    @pl.when(x == 3)
    def _():
        sg[2, 9] = zero_plane
        for f in (pf, af):
            for par in range(2):
                f[par, 2, 9] = zero_plane

    for d in range(2):
        @pl.when(y == 3 * d)
        def _():
            ysg[d, 0] = jnp.zeros((2, 8, 128), F32)
            for yf in (ypf, yaf):
                for par in range(2):
                    yf[par, d] = jnp.zeros((2, 8, 128), F32)
            for par in range(2):
                yct[par, d, 0] = jnp.zeros((8, 128), F32)

    barrier = pltpu.get_barrier_semaphore()

    def greet(where):
        pl.semaphore_signal(barrier, inc=1, device_id=where, device_id_type=MESH)

    def greet_row(k, carry):
        greet(dev(x, (y + k // 2) % 4, z, (c + k % 2) % 2))
        return carry

    def greet_plane(k, carry):
        greet(dev((x + 1 + k // 8) % 4, (k // 2) % 4, z, k % 2))
        return carry

    def greet_column(k, carry):
        greet(dev(x, y, (z + 1 + k // 2) % 16, k % 2))
        greet(dev(x, y, (z + 15 - k // 2) % 16, k % 2))
        return carry

    def greet_far(k, carry):
        greet(dev(x, (y + k) % 4, (z + 4) % 16, c))
        greet(dev(x, (y + k) % 4, (z + 12) % 16, c))
        return carry

    lax.fori_loop(0, 8, greet_column, 0)
    lax.fori_loop(1, 4, greet_far, 0)
    lax.fori_loop(1, 8, greet_row, 0)
    lax.fori_loop(0, 24, greet_plane, 0)

    fetched = [
        pltpu.make_async_copy(a, b, fetch.at[k])
        for k, (a, b) in enumerate(((vel, vbf), (contacts, cin), (sources, sin), (receivers, rin), (observed, oin)))
    ]
    for copy in fetched:
        copy.start()
    for copy in fetched:
        copy.wait()
    for d in range(3):
        for p in range(2):
            vf[d, p] = vbf[d, p].astype(F32)
    sub = iota((64, 128), 0)
    col = iota((64, 128), 1)
    cells = cin[...]
    q_at = jnp.zeros((16, 128), F32)
    l_at = jnp.zeros((16, 128), F32)
    for k in range(4):
        here = col[0:16] == sub[0:16] + 16 * k
        q_at = jnp.where(here, (cells[:, k : k + 1] // 128).astype(F32), q_at)
        l_at = jnp.where(here, (cells[:, k : k + 1] % 128).astype(F32), l_at)
    used = col[0:1] < 64
    q_row = jnp.where(used, jnp.sum(q_at, axis=0, keepdims=True), -1.0)
    l_row = jnp.where(used, jnp.sum(l_at, axis=0, keepdims=True), -1.0)
    msend[...] = jnp.zeros((2, 8, 128), F32)
    for j in range(2):
        msend[j, 0:1, :] = q_row
        msend[j, 1:2, :] = l_row
        pairs = rin[j].astype(F32)
        for k in range(2):
            at = jnp.where(sub == col, pairs[:, k : k + 1], 0.0)
            msend[j, 2 + k : 3 + k, :] = jnp.where(used, jnp.sum(at, axis=0, keepdims=True), -1.0)
            msend[j, 5 + k : 6 + k, :] = jnp.broadcast_to(sin[j : j + 1, k : k + 1].astype(F32), (1, 128))
        msend[j, 4:5, 0:64] = oin[j : j + 1, :]
    pl.semaphore_wait(barrier, 16 + 6 + 7 + 24)

    zz = (z + 8 * c) % 16
    home = zz < 8

    def landing(a, g):
        return ct.at[0, pl.ds(1 + 4 * g, 4)] if a == 0 else tv.at[a - 1, pl.ds(4 * g, 4)]

    def landing_two(a):
        return ct.at[0, pl.ds(1 + 2 * y, 2)] if a == 0 else tv.at[a - 1, pl.ds(2 * y, 2)]

    def in_rows(a, yt):
        rows = pl.ds(pl.multiple_of(32 * yt, 32), 32)
        return conc.at[:, rows] if a == 0 else poro.at[:, rows] if a == 4 else vf.at[a - 1, :, rows]

    def in_copy(a, d):
        yt = (y + d) % 4
        return remote(in_rows(a, yt), landing_two(a), in_s.at[a, d], in_r.at[a, y // 2], dev(x, yt, z, c))

    def in_local(a):
        return pltpu.make_async_copy(in_rows(a, y), landing_two(a), in_r.at[a, y // 2])

    @pl.when(home)
    def _():
        for a in range(5):
            for d in range(1, 4):
                in_copy(a, d).start()
            in_local(a).start()

    up = jnp.where((zz >= 7) & (zz <= 10), 1, 0)
    down = jnp.where((zz == 0) | (zz >= 13), 1, 0)
    zt = (z + up + 15 * down) % 16

    def relay(a, g):
        return remote(landing(a, g), landing(a, g), rel_s.at[a, g], in_r.at[a, g], dev(x, y, zt, c))

    def pass_on(a):
        for g in range(2):
            arrived(landing(a, g), in_r.at[a, g])

            @pl.when(up + down > 0)
            def _():
                relay(a, g).start()

    def passed_on(arrays):
        @pl.when(up + down > 0)
        def _():
            for a in arrays:
                for g in range(2):
                    relay(a, g).wait_send()

    def swap_copy(which, j, d):
        up4 = (j + zh + 1) % 2
        zt4 = (z + 4 * up4 + 12 * (1 - up4)) % 16
        yt = (y + d) % 4
        where = dev(x, yt, zt4, c)
        if which == 2:
            return remote(msend.at[j], mbuf.at[zh * 4 + y], sw_s.at[2, j, d], sw_r.at[2], where)
        src = (pot, adj)[which].at[j, :, pl.ds(pl.multiple_of(32 * yt, 32), 32)]
        dst = (pf, af)[which].at[0, 1 + zh, pl.ds(1 + 2 * y, 2)]
        return remote(src, dst, sw_s.at[which, j, d], sw_r.at[which], where)

    def swap_copies(which, j):
        return [swap_copy(which, j, d) for d in range(4)]

    def t_x(par):
        return [
            remote(ct.at[par, 8], ct.at[par, 10 * x_last * c], t_s.at[par, 0], t_r.at[par, 0],
                   dev(xn, y, z, (c + x_last) % 2)),
            remote(ct.at[par, 1], ct.at[par, 9 + 2 * x_first * (1 - c)], t_s.at[par, 1], t_r.at[par, 1],
                   dev(xp, y, z, (c + x_first) % 2)),
        ]

    def t_y(par):
        return [
            remote(yst.at[par, 0], yct.at[par, 0, 0], t_s.at[par, 2], t_r.at[par, 2], dev(x, yn, z, c)),
            remote(yst.at[par, 1], yct.at[par, 1, 0], t_s.at[par, 3], t_r.at[par, 3], dev(x, yp, z, c)),
        ]

    row = iota((32, 128), 0)
    lane = iota((32, 128), 1)

    def shift_y(v, low, high):
        below = jnp.where(row == 0, low, pltpu.roll(v, 1, 0))
        above = jnp.where(row == 31, high, pltpu.roll(v, 31, 0))
        return below, above

    def t_rows(par, p, v):
        yst[par, 0, p : p + 1, :] = v[31:32]
        yst[par, 1, p : p + 1, :] = v[0:1]

    pass_on(0)
    for copy in t_x(0):
        copy.start()
    for p in range(8):
        t_rows(0, p, ct[0, p + 1])
    start_y(t_y(0))
    for j in range(2):
        for copy in swap_copies(2, j):
            copy.start()
    for a in range(1, 4):
        pass_on(a)
        for d in range(4):
            if a < 3:
                swap_copy(0, a - 1, d).start()
    passed_on([0])

    def t_step(par, last):
        new = 1 - par

        def plane(p):
            v = ct[par, p + 1]
            xlow = ct[par, p]
            xhigh = ct[par, p + 2]
            ylow, yhigh = shift_y(v, yct[par, 0, 0, p : p + 1, :], yct[par, 1, 0, p : p + 1, :])
            zlow = jnp.where(lane == 0, 0.0, pltpu.roll(v, 1, 1))
            zhigh = jnp.where(lane == 127, 0.0, pltpu.roll(v, 127, 1))
            change = None
            for d, (low, high) in enumerate(((xlow, xhigh), (ylow, yhigh), (zlow, zhigh))):
                speed = tv[d, p]
                term = jnp.maximum(speed, 0.0) * (v - low) + jnp.minimum(speed, 0.0) * (high - v)
                change = term if change is None else change + term
            v = v - change
            ct[new, p + 1] = v
            t_rows(new, p, v)

        wait_y(t_y(par))
        for copy in t_x(par):
            copy.wait()
        plane(0)
        plane(7)

        @pl.when(jnp.logical_not(last))
        def _():
            for copy in t_x(new):
                copy.start()

        for p in range(1, 7):
            plane(p)

        @pl.when(jnp.logical_not(last))
        def _():
            start_y(t_y(new))

    def t_two(s, carry):
        t_step(0, s < 0)

        @pl.when(s == 0)
        def _():
            pass_on(4)

        @pl.when(s < 2)
        def _():
            swap_copy(1, s % 2, 0).start()
            swap_copy(1, s % 2, 1).start()

        t_step(1, s == STEPS // 2 - 1)

        @pl.when(s < 2)
        def _():
            swap_copy(1, s % 2, 2).start()
            swap_copy(1, s % 2, 3).start()

        return carry

    lax.fori_loop(0, STEPS // 2, t_two, 0)
    passed_on(range(1, 5))

    for p in range(8):
        v = jnp.exp(1.8 * jnp.log(tv[3, p])) * (0.5 + ct[0, p + 1])
        sg[1 + c, p + 1] = v
        yss[0, p : p + 1, :] = v[31:32]
        yss[1, p : p + 1, :] = v[0:1]

    def sg_x(cc):
        return [
            remote(sg.at[1 + c, 8], sg.at[1 + c + x_last, 0], sg_s.at[0, cc], sg_r.at[0, c], dev(xn, y, z, cc)),
            remote(sg.at[1 + c, 1], sg.at[1 + c - x_first, 9], sg_s.at[1, cc], sg_r.at[1, c], dev(xp, y, z, cc)),
        ]

    def sg_y(cc):
        return [
            remote(yss.at[0], ysg.at[0, 0, c], sg_s.at[2, cc], sg_r.at[2, c], dev(x, yn, z, cc)),
            remote(yss.at[1], ysg.at[1, 0, c], sg_s.at[3, cc], sg_r.at[3, c], dev(x, yp, z, cc)),
        ]

    tile_copy = remote(
        sg.at[1 + c, pl.ds(1, 8)], sg.at[1 + c, pl.ds(1, 8)], tile_s, tile_r, dev(x, y, z, 1 - c)
    )
    tile_copy.start()
    for cc in range(2):
        start_y(sg_y(cc))
        for copy in sg_x(cc):
            copy.start()

    arrived(mbuf, sw_r.at[2])

    def tables(k, carry):
        q = iota((64, 128), 0)
        target = ((q // 32) * 128 + q % 32 + 32 * y).astype(F32)
        rt[k] = jnp.where(target == mbuf[k, 0:1, :], 1.0, 0.0)
        lt[k] = jnp.where(iota((128, 128), 0).astype(F32) == mbuf[k, 1:2, :], 1.0, 0.0).astype(BF16)
        return carry

    lax.fori_loop(0, 8, tables, 0)
    jj = iota((128, 128), 0)
    mm = iota((128, 128), 1)
    spread = jnp.where((jj % 16 == mm % 16) & (mm < 64), 0.25, 0.0)
    own = jnp.where(iota((8, 128), 1) // 16 == iota((8, 128), 0), 1.0, 0.0)
    r0 = mbuf[0, 2:3, :]
    r1 = mbuf[0, 3:4, :]
    measured = mbuf[0, 4:5, :]
    ja = mbuf[0, 5:6, :]
    jb = mbuf[0, 6:7, :]

    tile_copy.wait()
    for cc in range(2):
        for d, copy in enumerate(sg_x(cc)):
            copy.wait_send()
            arrived(sg.at[1, 0], sg_r.at[d, cc])

        @pl.when(y < 3)
        def _():
            sg_y(cc)[0].wait_send()
            arrived(yss.at[0], sg_r.at[3, cc])

        @pl.when(y > 0)
        def _():
            sg_y(cc)[1].wait_send()
            arrived(yss.at[0], sg_r.at[2, cc])

    def faces_of(h, p):
        s = sg[1 + h, p + 1]
        low = ysg[0, 0, h, p : p + 1, :]
        high = ysg[1, 0, h, p : p + 1, :]
        _, syp = shift_y(s, low, high)
        szp = jnp.where(lane == 127, 0.0, pltpu.roll(s, 127, 1))
        ux = harmonic(s, sg[1 + h, p + 2])
        uy = harmonic(s, syp)
        uz = harmonic(s, szp)
        return s, low, ux, uy, uz

    for h in range(2):
        lx = harmonic(sg[1 + h, 0], sg[1 + h, 1])
        for p in range(8):
            s, low, ux, uy, uz = faces_of(h, p)
            ly = jnp.where(row == 0, harmonic(low, s[0:1]), pltpu.roll(uy, 1, 0))
            lz = pltpu.roll(uz, 1, 1)
            r = 0.8 / (ux + lx + uy + ly + uz + lz)
            rdiag[h, p] = r
            for k, face in enumerate((ux, lx, uy, ly, uz, lz)):
                coef[k, h, p] = face * r
            lx = ux

    def inject(current):
        vals = dot(jnp.broadcast_to(current, (8, 128)) * own, spread)
        for k in range(8):
            h, pair = k // 4, 2 * (k % 4)
            block = dot_t(rt[k] * vals[k : k + 1, :], lt[k])
            bsrc[h, pair] = block[0:32] * rdiag[h, pair]
            bsrc[h, pair + 1] = block[32:64] * rdiag[h, pair + 1]

    def field(f, yf, ysend, s_sem, r_sem):
        def x_copies(par):
            return [
                remote(f.at[par, pl.ds(1, 2), 8], f.at[par, pl.ds(1 + x_last, 2), 0],
                       s_sem.at[par, 0], r_sem.at[par, 0], dev(xn, y, z, c)),
                remote(f.at[par, pl.ds(1, 2), 1], f.at[par, pl.ds(1 - x_first, 2), 9],
                       s_sem.at[par, 1], r_sem.at[par, 1], dev(xp, y, z, c)),
            ]

        def y_copies(par):
            return [
                remote(ysend.at[par, 0], yf.at[par, 0], s_sem.at[par, 2], r_sem.at[par, 2], dev(x, yn, z, c)),
                remote(ysend.at[par, 1], yf.at[par, 1], s_sem.at[par, 3], r_sem.at[par, 3], dev(x, yp, z, c)),
            ]

        def edge_rows(par, h, p, v):
            ysend[par, 0, h, p : p + 1, :] = v[31:32]
            ysend[par, 1, h, p : p + 1, :] = v[0:1]

        def begin():
            for copy in x_copies(0):
                copy.start()
            for h in range(2):
                for p in range(8):
                    edge_rows(0, h, p, f[0, 1 + h, p + 1])
            start_y(y_copies(0))

        def end(par=0):
            wait_y(y_copies(par))
            for copy in x_copies(par):
                copy.wait()

        def sweep(par):
            new = 1 - par

            def plane(h, p):
                v = f[par, 1 + h, p + 1]
                ylow, yhigh = shift_y(v, yf[par, 0, h, p : p + 1, :], yf[par, 1, h, p : p + 1, :])
                out = coef[0, h, p] * f[par, 1 + h, p + 2] + coef[1, h, p] * f[par, 1 + h, p]
                out = out + (coef[2, h, p] * yhigh + coef[3, h, p] * ylow)
                out = out + (coef[4, h, p] * pltpu.roll(v, 127, 1) + coef[5, h, p] * pltpu.roll(v, 1, 1))
                out = (0.2 * v + bsrc[h, p]) + out
                f[new, 1 + h, p + 1] = out
                edge_rows(new, h, p, out)

            end(par)
            for p in (0, 7):
                for h in range(2):
                    plane(h, p)
            for copy in x_copies(new):
                copy.start()
            for h in range(2):
                for p in range(1, 7):
                    plane(h, p)
            start_y(y_copies(new))

        def two(s, carry):
            sweep(0)
            sweep(1)
            return carry

        def sweeps():
            lax.fori_loop(0, RELAX_SWEEPS // 2, two, 0)

        return begin, sweeps, end

    def electrode_ids(x_):
        j = iota((128, 128), 0)
        return ((j // 64) * 256 + x_ * 64 + j % 64).astype(F32)

    own_lane = iota((1, 128), 1)
    own_ids = ((own_lane // 64) * 256 + x * 64 + own_lane % 64).astype(F32)
    inject(4.0 * (jnp.where(own_ids == ja, 1.0, 0.0) - jnp.where(own_ids == jb, 1.0, 0.0)))

    p_begin, p_sweeps, p_end = field(pf, ypf, ypsend, p_s, p_r)
    a_begin, a_sweeps, a_end = field(af, yaf, yasend, a_s, a_r)
    arrived(pf.at[0, pl.ds(1, 2), pl.ds(1, 8)], sw_r.at[0])
    p_begin()
    p_sweeps()

    for k in range(8):
        h, pair = k // 4, 2 * (k % 4)
        block = pf[0, 1 + h, pl.ds(1 + pair, 2)].reshape(64, 128)
        vb[k : k + 1, :] = jnp.sum(rt[k] * dot(block, lt[k]), axis=0, keepdims=True)
    part = jnp.sum(dot_t(vb[...], spread) * own, axis=0, keepdims=True)
    vsend[...] = jnp.broadcast_to(part, (8, 128))

    def v_copy(k):
        xt = (x + k // 4) % 4
        yt = (y + k % 4) % 4
        return remote(vsend, vall.at[x * 4 + y], v_s.at[k], v_r, dev(xt, yt, z, c))

    for k in range(1, 16):
        v_copy(k).start()
    pltpu.make_async_copy(vsend, vall.at[x * 4 + y], v_r).start()
    arrived(af.at[0, pl.ds(1, 2), pl.ds(1, 8)], sw_r.at[1])
    a_begin()
    arrived(vall, v_r)

    def selector(x_):
        ids = electrode_ids(x_)
        return jnp.where(ids == r0, 1.0, 0.0) - jnp.where(ids == r1, 1.0, 0.0)

    readings = jnp.zeros((8, 128), F32)
    for k in range(4):
        volts = vall[4 * k] + vall[4 * k + 1] + vall[4 * k + 2] + vall[4 * k + 3]
        readings = readings + dot(volts, selector(k))
    rsend[...] = readings
    survey = (1 + zh + zl // 4) % 2

    def read_copies():
        return [
            remote(rsend, rdin.at[survey], rd_s.at[half], rd_r, dev(x, y, half * 8 + (zl + 4) % 8, c))
            for half in range(2)
        ]

    for copy in read_copies():
        copy.start()
    inject(dot_t(readings - measured, selector(x))[0:1])
    a_sweeps()
    p_end()
    a_end()

    def terms(h, p):
        _, _, ux, uy, uz = faces_of(h, p)
        pv = pf[0, 1 + h, p + 1]
        av = af[0, 1 + h, p + 1]
        _, py = shift_y(pv, pv[0:1], ypf[0, 1, h, p : p + 1, :])
        _, ay = shift_y(av, av[0:1], yaf[0, 1, h, p : p + 1, :])
        out = ux * (pf[0, 1 + h, p + 2] - pv) * (af[0, 1 + h, p + 2] - av)
        out = out + uy * (py - pv) * (ay - av)
        out = out + uz * (pltpu.roll(pv, 127, 1) - pv) * (pltpu.roll(av, 127, 1) - av)
        return -out

    def other(p):
        return remote(gbuf.at[p], grx.at[p], gx_s.at[p], gx_r.at[p], dev(x, y, z, 1 - c))

    def rs_copy(k, local):
        p, rh = k // 2, k % 2
        src = gsum.at[p, pl.ds(16 * rh, 16)]
        dst = rsbuf.at[z]
        if local:
            return pltpu.make_async_copy(src, dst, rs_r)
        return remote(src, dst, rs_s.at[k], rs_r, dev(x, y, 8 * c + p, rh))

    def rs_self(k):
        return (z == 8 * c + k // 2) & (c == k % 2)

    for p in range(8):
        gbuf[p] = terms(1 - c, p)
        other(p).start()
    for p in range(8):
        mine = terms(c, p)
        other(p).wait()
        gsum[p] = mine + grx[p]
        for k in (2 * p, 2 * p + 1):
            @pl.when(jnp.logical_not(rs_self(k)))
            def _():
                rs_copy(k, False).start()

            @pl.when(rs_self(k))
            def _():
                rs_copy(k, True).start()

    arrived(rsbuf, rs_r)
    added = rsbuf[0]
    for k in range(1, 16):
        added = added + rsbuf[k]
    osum[...] = added

    def ag_copy(k, local):
        dst = grad.at[zl % 2, pl.ds(pl.multiple_of(32 * y + 16 * c, 16), 16)]
        if local:
            return pltpu.make_async_copy(osum, dst, ag_r)
        return remote(osum, dst, ag_s.at[k], ag_r, dev(x, zl // 2, 8 * zh + k // 2, k % 2))

    def ag_self(k):
        return (y == zl // 2) & (zl == k // 2) & (c == k % 2)

    for k in range(16):
        @pl.when(jnp.logical_not(ag_self(k)))
        def _():
            ag_copy(k, False).start()

        @pl.when(ag_self(k))
        def _():
            ag_copy(k, True).start()

    arrived(rdin, rd_r)
    read[0:1, :] = rdin[0, 0:1, 0:64]
    read[1:2, :] = rdin[1, 0:1, 0:64]
    arrived(grad, ag_r)

    @pl.when(home)
    def _():
        for a in range(5):
            for d in range(1, 4):
                in_copy(a, d).wait_send()

    for which in range(3):
        for j in range(2):
            for copy in swap_copies(which, j):
                copy.wait_send()
    for k in range(1, 16):
        v_copy(k).wait_send()
    for copy in read_copies():
        copy.wait_send()
    for k in range(16):
        @pl.when(jnp.logical_not(rs_self(k)))
        def _():
            rs_copy(k, False).wait_send()

        @pl.when(jnp.logical_not(ag_self(k)))
        def _():
            ag_copy(k, False).wait_send()


def on_device(
    concentration, velocity, porosity, contacts, sources, receivers, observed, potential_init, adjoint_init
):
    V = pltpu.VMEM
    D = pltpu.SemaphoreType.DMA
    scratch = [
        V((2, 12, 32, 128), F32), V((2, 2, 2, 8, 128), F32), V((2, 2, 8, 128), F32), V((4, 8, 32, 128), F32),
        V((4, 10, 32, 128), F32), V((2, 2, 2, 8, 128), F32), V((2, 8, 128), F32),
        V((6, 2, 8, 32, 128), F32), V((2, 8, 32, 128), F32), V((2, 8, 32, 128), F32),
        V((2, 4, 10, 32, 128), F32), V((2, 2, 2, 8, 128), F32), V((2, 2, 2, 8, 128), F32),
        V((2, 4, 10, 32, 128), F32), V((2, 2, 2, 8, 128), F32), V((2, 2, 2, 8, 128), F32),
        V((8, 8, 128), F32), V((8, 64, 128), F32), V((8, 128, 128), BF16), V((8, 128), F32), V((8, 128), F32),
        V((16, 8, 128), F32), V((8, 128), F32), V((2, 8, 128), F32),
        V((8, 32, 128), F32), V((8, 32, 128), F32), V((8, 32, 128), F32), V((16, 16, 128), F32), V((16, 128), F32),
        V((3, 2, 128, 128), BF16), V((3, 2, 128, 128), F32), V((16, 4), jnp.int32), V((2, 2), jnp.int32),
        V((2, 64, 2), jnp.int32), V((2, 64), F32), V((2, 8, 128), F32),
        D((5, 4)), D((5, 2)), D((5, 2)), D((2, 4)), D((2, 4)), D((3, 2, 4)), D((3,)), D((4, 2)), D((4, 2)), D, D,
        D((2, 4)), D((2, 4)), D((2, 4)), D((2, 4)), D((16,)), D, D((2,)), D, D((8,)), D((8,)), D((16,)), D, D((16,)), D,
        D((5,)),
    ]
    gradient, readings = pl.pallas_call(
        kernel,
        out_shape=(jax.ShapeDtypeStruct((2, 128, 128), F32), jax.ShapeDtypeStruct((2, 64), F32)),
        in_specs=[pl.BlockSpec(memory_space=pl.ANY)] * 9,
        out_specs=(pl.BlockSpec(memory_space=pltpu.VMEM), pl.BlockSpec(memory_space=pltpu.VMEM)),
        scratch_shapes=scratch,
        compiler_params=pltpu.CompilerParams(collective_id=0, has_side_effects=True),
        name="survey_gradient",
    )(
        concentration, velocity, porosity, contacts, sources, receivers, observed, potential_init, adjoint_init
    )
    return gradient, readings


def solution(mesh):
    return jax.shard_map(
        on_device,
        mesh=mesh,
        in_specs=(
            P("space", None, None),
            P(None, "space", None, None),
            P("space", None, None),
            P("space", None),
            P("tm", None),
            P("tm", None, None),
            P("tm", None),
            P("tm", "space", None, None),
            P("tm", "space", None, None),
        ),
        out_specs=(P("space", None, None), P("tm", None)),
        check_vma=False,
    )
```

```python
import jax
import jax.numpy as jnp
from jax import lax
from jax.experimental import pallas as pl
from jax.experimental.pallas import tpu as pltpu
from jax.sharding import PartitionSpec as P

STEPS = 8
RELAX_SWEEPS = 6
MESH = pl.DeviceIdType.MESH
F32 = jnp.float32
BF16 = jnp.bfloat16


def harmonic(first, second):
    return 2.0 * (first * second) / (first + second)


def iota(shape, dim):
    return lax.broadcasted_iota(jnp.int32, shape, dim)


def parts(a):
    high = a.astype(BF16)
    rest = a - high.astype(F32)
    middle = rest.astype(BF16)
    low = (rest - middle.astype(F32)).astype(BF16)
    return jnp.concatenate([high, middle, low], axis=0)


def total(product):
    rows = product.shape[0] // 3
    return product[:rows] + (product[rows : 2 * rows] + product[2 * rows :])


def dot(a, exact):
    dims = (((1,), (0,)), ((), ()))
    return total(lax.dot_general(parts(a), exact.astype(BF16), dims, preferred_element_type=F32))


def dot_t(a, exact):
    dims = (((1,), (1,)), ((), ()))
    return total(lax.dot_general(parts(a), exact.astype(BF16), dims, preferred_element_type=F32))


def kernel(
    conc, vel, poro, contacts, sources, receivers, observed, pot, adj, grad, read,
    ct, yct, yst, tv, sg, ysg, yss, coef, rdiag, bsrc,
    pf, ypf, ypsend, af, yaf, yasend,
    mbuf, rt, lt, vb, vsend, vall, rsend, rdin,
    gbuf, grx, gsum, rsbuf, osum, vbf, vf, cin, sin, rin, oin, msend,
    in_s, in_r, rel_s, t_s, t_r, sw_s, sw_r, sg_s, sg_r, tile_s, tile_r,
    p_s, p_r, a_s, a_r, v_s, v_r, rd_s, rd_r, gx_s, gx_r, rs_s, rs_r, ag_s, ag_r, fetch,
):
    space = lax.axis_index("space")
    tm = lax.axis_index("tm")
    zh = space // 16
    x = (space // 4) % 4
    y = space % 4
    zl = tm // 2
    c = tm % 2
    z = zh * 8 + zl

    def dev(x_, y_, z_, c_):
        return {"space": (z_ // 8) * 16 + x_ * 4 + y_, "tm": (z_ % 8) * 2 + c_}

    def remote(src, dst, s, r, where):
        return pltpu.make_async_remote_copy(
            src_ref=src, dst_ref=dst, send_sem=s, recv_sem=r, device_id=where, device_id_type=MESH
        )

    def arrived(ref, sem):
        pltpu.make_async_copy(ref, ref, sem).wait()

    def start_y(copies):
        @pl.when(y < 3)
        def _():
            copies[0].start()

        @pl.when(y > 0)
        def _():
            copies[1].start()

    def wait_y(copies):
        @pl.when(y < 3)
        def _():
            copies[0].wait_send()
            copies[1].wait_recv()

        @pl.when(y > 0)
        def _():
            copies[1].wait_send()
            copies[0].wait_recv()

    xn = (x + 1) % 4
    xp = (x + 3) % 4
    yn = (y + 1) % 4
    yp = (y + 3) % 4
    x_last = (x + 1) // 4
    x_first = (3 - x) // 3

    zero_plane = jnp.zeros((32, 128), F32)

    @pl.when((x == 0) & (c == 0))
    def _():
        for par in range(2):
            ct[par, 0] = zero_plane

    @pl.when((x == 3) & (c == 1))
    def _():
        for par in range(2):
            ct[par, 9] = zero_plane

    @pl.when(x == 0)
    def _():
        sg[1, 0] = zero_plane
        for f in (pf, af):
            for par in range(2):
                f[par, 1, 0] = zero_plane

    @pl.when(x == 3)
    def _():
        sg[2, 9] = zero_plane
        for f in (pf, af):
            for par in range(2):
                f[par, 2, 9] = zero_plane

    for d in range(2):
        @pl.when(y == 3 * d)
        def _():
            ysg[d, 0] = jnp.zeros((2, 8, 128), F32)
            for yf in (ypf, yaf):
                for par in range(2):
                    yf[par, d] = jnp.zeros((2, 8, 128), F32)
            for par in range(2):
                yct[par, d, 0] = jnp.zeros((8, 128), F32)

    barrier = pltpu.get_barrier_semaphore()

    def greet(where):
        pl.semaphore_signal(barrier, inc=1, device_id=where, device_id_type=MESH)

    def greet_row(k, carry):
        greet(dev(x, (y + k // 2) % 4, z, (c + k % 2) % 2))
        return carry

    def greet_plane(k, carry):
        greet(dev((x + 1 + k // 8) % 4, (k // 2) % 4, z, k % 2))
        return carry

    def greet_column(k, carry):
        greet(dev(x, y, (z + 1 + k // 2) % 16, k % 2))
        greet(dev(x, y, (z + 15 - k // 2) % 16, k % 2))
        return carry

    def greet_far(k, carry):
        greet(dev(x, (y + k) % 4, (z + 4) % 16, c))
        greet(dev(x, (y + k) % 4, (z + 12) % 16, c))
        return carry

    lax.fori_loop(0, 8, greet_column, 0)
    lax.fori_loop(1, 4, greet_far, 0)
    lax.fori_loop(1, 8, greet_row, 0)
    lax.fori_loop(0, 24, greet_plane, 0)

    fetched = [
        pltpu.make_async_copy(a, b, fetch.at[k])
        for k, (a, b) in enumerate(((vel, vbf), (contacts, cin), (sources, sin), (receivers, rin), (observed, oin)))
    ]
    for copy in fetched:
        copy.start()
    for copy in fetched:
        copy.wait()
    for d in range(3):
        for p in range(2):
            vf[d, p] = vbf[d, p].astype(F32)
    cells = cin[...]
    msend[...] = jnp.zeros((2, 8, 128), F32)
    for j in range(2):
        msend[j, 0:4, :] = jnp.full((4, 128), -1.0, F32)
        for k in range(4):
            msend[j, 0:1, 16 * k : 16 * k + 16] = (cells[k : k + 1] // 128).astype(F32)
            msend[j, 1:2, 16 * k : 16 * k + 16] = (cells[k : k + 1] % 128).astype(F32)
        for k in range(2):
            msend[j, 2 + k : 3 + k, 0:64] = rin[j, k : k + 1, :].astype(F32)
            msend[j, 5 + k : 6 + k, :] = jnp.broadcast_to(sin[j : j + 1, k : k + 1].astype(F32), (1, 128))
        msend[j, 4:5, 0:64] = oin[j : j + 1, :]
    pl.semaphore_wait(barrier, 16 + 6 + 7 + 24)

    zz = (z + 8 * c) % 16
    home = zz < 8

    def swap_copy(which, j, d):
        up4 = (j + zh + 1) % 2
        zt4 = (z + 4 * up4 + 12 * (1 - up4)) % 16
        yt = (y + d) % 4
        where = dev(x, yt, zt4, c)
        if which == 2:
            return remote(msend.at[j], mbuf.at[zh * 4 + y], sw_s.at[2, j, d], sw_r.at[2], where)
        src = (pot, adj)[which].at[j, :, pl.ds(pl.multiple_of(32 * yt, 32), 32)]
        dst = (pf, af)[which].at[0, 1 + zh, pl.ds(1 + 2 * y, 2)]
        return remote(src, dst, sw_s.at[which, j, d], sw_r.at[which], where)

    def swap_copies(which, j):
        return [swap_copy(which, j, d) for d in range(4)]

    def landing(a, g):
        return ct.at[0, pl.ds(1 + 4 * g, 4)] if a == 0 else tv.at[a - 1, pl.ds(4 * g, 4)]

    def landing_two(a):
        return ct.at[0, pl.ds(1 + 2 * y, 2)] if a == 0 else tv.at[a - 1, pl.ds(2 * y, 2)]

    def in_rows(a, yt):
        rows = pl.ds(pl.multiple_of(32 * yt, 32), 32)
        return conc.at[:, rows] if a == 0 else poro.at[:, rows] if a == 4 else vf.at[a - 1, :, rows]

    def in_copy(a, d):
        yt = (y + d) % 4
        return remote(in_rows(a, yt), landing_two(a), in_s.at[a, d], in_r.at[a, y // 2], dev(x, yt, z, c))

    def in_local(a):
        return pltpu.make_async_copy(in_rows(a, y), landing_two(a), in_r.at[a, y // 2])

    @pl.when(home)
    def _():
        for a in range(5):
            for d in range(1, 4):
                in_copy(a, d).start()
            in_local(a).start()

    for j in range(2):
        for d in range(4):
            swap_copy(0, j, d).start()

    up = jnp.where((zz >= 7) & (zz <= 10), 1, 0)
    down = jnp.where((zz == 0) | (zz >= 13), 1, 0)
    zt = (z + up + 15 * down) % 16

    def relay(a, g):
        return remote(landing(a, g), landing(a, g), rel_s.at[a, g], in_r.at[a, g], dev(x, y, zt, c))

    def pass_on(a):
        for g in range(2):
            arrived(landing(a, g), in_r.at[a, g])

            @pl.when(up + down > 0)
            def _():
                relay(a, g).start()

    def passed_on(arrays):
        @pl.when(up + down > 0)
        def _():
            for a in arrays:
                for g in range(2):
                    relay(a, g).wait_send()

    def t_x(par):
        return [
            remote(ct.at[par, 8], ct.at[par, 10 * x_last * c], t_s.at[par, 0], t_r.at[par, 0],
                   dev(xn, y, z, (c + x_last) % 2)),
            remote(ct.at[par, 1], ct.at[par, 9 + 2 * x_first * (1 - c)], t_s.at[par, 1], t_r.at[par, 1],
                   dev(xp, y, z, (c + x_first) % 2)),
        ]

    def t_y(par):
        return [
            remote(yst.at[par, 0], yct.at[par, 0, 0], t_s.at[par, 2], t_r.at[par, 2], dev(x, yn, z, c)),
            remote(yst.at[par, 1], yct.at[par, 1, 0], t_s.at[par, 3], t_r.at[par, 3], dev(x, yp, z, c)),
        ]

    row = iota((32, 128), 0)
    lane = iota((32, 128), 1)

    def shift_y(v, low, high):
        below = jnp.where(row == 0, low, pltpu.roll(v, 1, 0))
        above = jnp.where(row == 31, high, pltpu.roll(v, 31, 0))
        return below, above

    def t_rows(par, p, v):
        yst[par, 0, p : p + 1, :] = v[31:32]
        yst[par, 1, p : p + 1, :] = v[0:1]

    pass_on(0)
    for copy in t_x(0):
        copy.start()
    for p in range(8):
        t_rows(0, p, ct[0, p + 1])
    start_y(t_y(0))
    for j in range(2):
        for copy in swap_copies(2, j):
            copy.start()
    for a in range(1, 4):
        pass_on(a)
    passed_on([0])

    def t_step(par, last):
        new = 1 - par

        def plane(p):
            v = ct[par, p + 1]
            xlow = ct[par, p]
            xhigh = ct[par, p + 2]
            ylow, yhigh = shift_y(v, yct[par, 0, 0, p : p + 1, :], yct[par, 1, 0, p : p + 1, :])
            zlow = jnp.where(lane == 0, 0.0, pltpu.roll(v, 1, 1))
            zhigh = jnp.where(lane == 127, 0.0, pltpu.roll(v, 127, 1))
            change = None
            for d, (low, high) in enumerate(((xlow, xhigh), (ylow, yhigh), (zlow, zhigh))):
                speed = tv[d, p]
                term = jnp.maximum(speed, 0.0) * (v - low) + jnp.minimum(speed, 0.0) * (high - v)
                change = term if change is None else change + term
            v = v - change
            ct[new, p + 1] = v
            t_rows(new, p, v)

        wait_y(t_y(par))
        for copy in t_x(par):
            copy.wait()
        plane(0)
        plane(7)

        @pl.when(jnp.logical_not(last))
        def _():
            for copy in t_x(new):
                copy.start()

        for p in range(1, 7):
            plane(p)

        @pl.when(jnp.logical_not(last))
        def _():
            start_y(t_y(new))

    def t_two(s, carry):
        t_step(0, s < 0)

        @pl.when(s == 0)
        def _():
            pass_on(4)

        t_step(1, s == STEPS // 2 - 1)

        return carry

    lax.fori_loop(0, STEPS // 2, t_two, 0)
    passed_on(range(1, 5))

    for p in range(8):
        v = jnp.exp(1.8 * jnp.log(tv[3, p])) * (0.5 + ct[0, p + 1])
        sg[1 + c, p + 1] = v
        yss[0, p : p + 1, :] = v[31:32]
        yss[1, p : p + 1, :] = v[0:1]

    def sg_x(cc):
        return [
            remote(sg.at[1 + c, 8], sg.at[1 + c + x_last, 0], sg_s.at[0, cc], sg_r.at[0, c], dev(xn, y, z, cc)),
            remote(sg.at[1 + c, 1], sg.at[1 + c - x_first, 9], sg_s.at[1, cc], sg_r.at[1, c], dev(xp, y, z, cc)),
        ]

    def sg_y(cc):
        return [
            remote(yss.at[0], ysg.at[0, 0, c], sg_s.at[2, cc], sg_r.at[2, c], dev(x, yn, z, cc)),
            remote(yss.at[1], ysg.at[1, 0, c], sg_s.at[3, cc], sg_r.at[3, c], dev(x, yp, z, cc)),
        ]

    tile_copy = remote(
        sg.at[1 + c, pl.ds(1, 8)], sg.at[1 + c, pl.ds(1, 8)], tile_s, tile_r, dev(x, y, z, 1 - c)
    )
    tile_copy.start()
    for cc in range(2):
        start_y(sg_y(cc))
        for copy in sg_x(cc):
            copy.start()
    for j in range(2):
        for d in range(4):
            swap_copy(1, j, d).start()

    arrived(mbuf, sw_r.at[2])

    def tables(k, carry):
        q = iota((64, 128), 0)
        target = ((q // 32) * 128 + q % 32 + 32 * y).astype(F32)
        rt[k] = jnp.where(target == mbuf[k, 0:1, :], 1.0, 0.0)
        lt[k] = jnp.where(iota((128, 128), 0).astype(F32) == mbuf[k, 1:2, :], 1.0, 0.0).astype(BF16)
        return carry

    lax.fori_loop(0, 8, tables, 0)
    jj = iota((128, 128), 0)
    mm = iota((128, 128), 1)
    spread = jnp.where((jj % 16 == mm % 16) & (mm < 64), 0.25, 0.0)
    own = jnp.where(iota((8, 128), 1) // 16 == iota((8, 128), 0), 1.0, 0.0)
    r0 = mbuf[0, 2:3, :]
    r1 = mbuf[0, 3:4, :]
    measured = mbuf[0, 4:5, :]
    ja = mbuf[0, 5:6, :]
    jb = mbuf[0, 6:7, :]

    tile_copy.wait()
    for cc in range(2):
        for d, copy in enumerate(sg_x(cc)):
            copy.wait_send()
            arrived(sg.at[1, 0], sg_r.at[d, cc])

        @pl.when(y < 3)
        def _():
            sg_y(cc)[0].wait_send()
            arrived(yss.at[0], sg_r.at[3, cc])

        @pl.when(y > 0)
        def _():
            sg_y(cc)[1].wait_send()
            arrived(yss.at[0], sg_r.at[2, cc])

    def faces_of(h, p):
        s = sg[1 + h, p + 1]
        low = ysg[0, 0, h, p : p + 1, :]
        high = ysg[1, 0, h, p : p + 1, :]
        _, syp = shift_y(s, low, high)
        szp = jnp.where(lane == 127, 0.0, pltpu.roll(s, 127, 1))
        ux = harmonic(s, sg[1 + h, p + 2])
        uy = harmonic(s, syp)
        uz = harmonic(s, szp)
        return s, low, ux, uy, uz

    for h in range(2):
        lx = harmonic(sg[1 + h, 0], sg[1 + h, 1])
        for p in range(8):
            s, low, ux, uy, uz = faces_of(h, p)
            ly = jnp.where(row == 0, harmonic(low, s[0:1]), pltpu.roll(uy, 1, 0))
            lz = pltpu.roll(uz, 1, 1)
            r = 0.8 / (ux + lx + uy + ly + uz + lz)
            rdiag[h, p] = r
            for k, face in enumerate((ux, lx, uy, ly, uz, lz)):
                coef[k, h, p] = face * r
            lx = ux

    def inject(current):
        vals = dot(jnp.broadcast_to(current, (8, 128)) * own, spread)
        for k in range(8):
            h, pair = k // 4, 2 * (k % 4)
            block = dot_t(rt[k] * vals[k : k + 1, :], lt[k])
            bsrc[h, pair] = block[0:32] * rdiag[h, pair]
            bsrc[h, pair + 1] = block[32:64] * rdiag[h, pair + 1]

    def field(f, yf, ysend, s_sem, r_sem):
        def x_copies(par):
            return [
                remote(f.at[par, pl.ds(1, 2), 8], f.at[par, pl.ds(1 + x_last, 2), 0],
                       s_sem.at[par, 0], r_sem.at[par, 0], dev(xn, y, z, c)),
                remote(f.at[par, pl.ds(1, 2), 1], f.at[par, pl.ds(1 - x_first, 2), 9],
                       s_sem.at[par, 1], r_sem.at[par, 1], dev(xp, y, z, c)),
            ]

        def y_copies(par):
            return [
                remote(ysend.at[par, 0], yf.at[par, 0], s_sem.at[par, 2], r_sem.at[par, 2], dev(x, yn, z, c)),
                remote(ysend.at[par, 1], yf.at[par, 1], s_sem.at[par, 3], r_sem.at[par, 3], dev(x, yp, z, c)),
            ]

        def edge_rows(par, h, p, v):
            ysend[par, 0, h, p : p + 1, :] = v[31:32]
            ysend[par, 1, h, p : p + 1, :] = v[0:1]

        def begin():
            for copy in x_copies(0):
                copy.start()
            for h in range(2):
                for p in range(8):
                    edge_rows(0, h, p, f[0, 1 + h, p + 1])
            start_y(y_copies(0))

        def end(par=0):
            wait_y(y_copies(par))
            for copy in x_copies(par):
                copy.wait()

        def sweep(par):
            new = 1 - par

            def plane(h, p):
                v = f[par, 1 + h, p + 1]
                ylow, yhigh = shift_y(v, yf[par, 0, h, p : p + 1, :], yf[par, 1, h, p : p + 1, :])
                out = coef[0, h, p] * f[par, 1 + h, p + 2] + coef[1, h, p] * f[par, 1 + h, p]
                out = out + (coef[2, h, p] * yhigh + coef[3, h, p] * ylow)
                out = out + (coef[4, h, p] * pltpu.roll(v, 127, 1) + coef[5, h, p] * pltpu.roll(v, 1, 1))
                out = (0.2 * v + bsrc[h, p]) + out
                f[new, 1 + h, p + 1] = out
                edge_rows(new, h, p, out)

            end(par)
            for p in (0, 7):
                for h in range(2):
                    plane(h, p)
            for copy in x_copies(new):
                copy.start()
            for h in range(2):
                for p in range(1, 7):
                    plane(h, p)
            start_y(y_copies(new))

        def two(s, carry):
            sweep(0)
            sweep(1)
            return carry

        def sweeps():
            lax.fori_loop(0, RELAX_SWEEPS // 2, two, 0)

        return begin, sweeps, end

    def electrode_ids(x_):
        j = iota((128, 128), 0)
        return ((j // 64) * 256 + x_ * 64 + j % 64).astype(F32)

    own_lane = iota((1, 128), 1)
    own_ids = ((own_lane // 64) * 256 + x * 64 + own_lane % 64).astype(F32)
    inject(4.0 * (jnp.where(own_ids == ja, 1.0, 0.0) - jnp.where(own_ids == jb, 1.0, 0.0)))

    p_begin, p_sweeps, p_end = field(pf, ypf, ypsend, p_s, p_r)
    a_begin, a_sweeps, a_end = field(af, yaf, yasend, a_s, a_r)
    arrived(pf.at[0, pl.ds(1, 2), pl.ds(1, 8)], sw_r.at[0])
    p_begin()
    p_sweeps()

    for k in range(8):
        h, pair = k // 4, 2 * (k % 4)
        block = pf[0, 1 + h, pl.ds(1 + pair, 2)].reshape(64, 128)
        vb[k : k + 1, :] = jnp.sum(rt[k] * dot(block, lt[k]), axis=0, keepdims=True)
    part = jnp.sum(dot_t(vb[...], spread) * own, axis=0, keepdims=True)
    vsend[...] = jnp.broadcast_to(part, (8, 128))

    def v_copy(k):
        xt = (x + k // 4) % 4
        yt = (y + k % 4) % 4
        return remote(vsend, vall.at[x * 4 + y], v_s.at[k], v_r, dev(xt, yt, z, c))

    for k in range(1, 16):
        v_copy(k).start()
    pltpu.make_async_copy(vsend, vall.at[x * 4 + y], v_r).start()
    arrived(af.at[0, pl.ds(1, 2), pl.ds(1, 8)], sw_r.at[1])
    a_begin()
    arrived(vall, v_r)

    def selector(x_):
        ids = electrode_ids(x_)
        return jnp.where(ids == r0, 1.0, 0.0) - jnp.where(ids == r1, 1.0, 0.0)

    readings = jnp.zeros((8, 128), F32)
    for k in range(4):
        volts = vall[4 * k] + vall[4 * k + 1] + vall[4 * k + 2] + vall[4 * k + 3]
        readings = readings + dot(volts, selector(k))
    rsend[...] = readings
    survey = (1 + zh + zl // 4) % 2

    def read_copies():
        return [
            remote(rsend, rdin.at[survey], rd_s.at[half], rd_r, dev(x, y, half * 8 + (zl + 4) % 8, c))
            for half in range(2)
        ]

    for copy in read_copies():
        copy.start()
    inject(dot_t(readings - measured, selector(x))[0:1])
    a_sweeps()
    p_end()
    a_end()

    def terms(h, p):
        _, _, ux, uy, uz = faces_of(h, p)
        pv = pf[0, 1 + h, p + 1]
        av = af[0, 1 + h, p + 1]
        _, py = shift_y(pv, pv[0:1], ypf[0, 1, h, p : p + 1, :])
        _, ay = shift_y(av, av[0:1], yaf[0, 1, h, p : p + 1, :])
        out = ux * (pf[0, 1 + h, p + 2] - pv) * (af[0, 1 + h, p + 2] - av)
        out = out + uy * (py - pv) * (ay - av)
        out = out + uz * (pltpu.roll(pv, 127, 1) - pv) * (pltpu.roll(av, 127, 1) - av)
        return -out

    def other(p):
        return remote(gbuf.at[p], grx.at[p], gx_s.at[p], gx_r.at[p], dev(x, y, z, 1 - c))

    def rs_copy(k, local):
        p, rh = k // 2, k % 2
        src = gsum.at[p, pl.ds(16 * rh, 16)]
        dst = rsbuf.at[z]
        if local:
            return pltpu.make_async_copy(src, dst, rs_r)
        return remote(src, dst, rs_s.at[k], rs_r, dev(x, y, 8 * c + p, rh))

    def rs_self(k):
        return (z == 8 * c + k // 2) & (c == k % 2)

    for p in range(8):
        gbuf[p] = terms(1 - c, p)
        other(p).start()
    for p in range(8):
        mine = terms(c, p)
        other(p).wait()
        gsum[p] = mine + grx[p]
        for k in (2 * p, 2 * p + 1):
            @pl.when(jnp.logical_not(rs_self(k)))
            def _():
                rs_copy(k, False).start()

            @pl.when(rs_self(k))
            def _():
                rs_copy(k, True).start()

    arrived(rsbuf, rs_r)
    added = rsbuf[0]
    for k in range(1, 16):
        added = added + rsbuf[k]
    osum[...] = added

    def ag_copy(k, local):
        dst = grad.at[zl % 2, pl.ds(pl.multiple_of(32 * y + 16 * c, 16), 16)]
        if local:
            return pltpu.make_async_copy(osum, dst, ag_r)
        return remote(osum, dst, ag_s.at[k], ag_r, dev(x, zl // 2, 8 * zh + k // 2, k % 2))

    def ag_self(k):
        return (y == zl // 2) & (zl == k // 2) & (c == k % 2)

    for k in range(16):
        @pl.when(jnp.logical_not(ag_self(k)))
        def _():
            ag_copy(k, False).start()

        @pl.when(ag_self(k))
        def _():
            ag_copy(k, True).start()

    arrived(rdin, rd_r)
    read[0:1, :] = rdin[0, 0:1, 0:64]
    read[1:2, :] = rdin[1, 0:1, 0:64]
    arrived(grad, ag_r)

    @pl.when(home)
    def _():
        for a in range(5):
            for d in range(1, 4):
                in_copy(a, d).wait_send()

    for which in range(3):
        for j in range(2):
            for copy in swap_copies(which, j):
                copy.wait_send()
    for k in range(1, 16):
        v_copy(k).wait_send()
    for copy in read_copies():
        copy.wait_send()
    for k in range(16):
        @pl.when(jnp.logical_not(rs_self(k)))
        def _():
            rs_copy(k, False).wait_send()

        @pl.when(jnp.logical_not(ag_self(k)))
        def _():
            ag_copy(k, False).wait_send()


def on_device(
    concentration, velocity, porosity, contacts, sources, receivers, observed, potential_init, adjoint_init
):
    V = pltpu.VMEM
    D = pltpu.SemaphoreType.DMA
    scratch = [
        V((2, 12, 32, 128), F32), V((2, 2, 2, 8, 128), F32), V((2, 2, 8, 128), F32), V((4, 8, 32, 128), F32),
        V((4, 10, 32, 128), F32), V((2, 2, 2, 8, 128), F32), V((2, 8, 128), F32),
        V((6, 2, 8, 32, 128), F32), V((2, 8, 32, 128), F32), V((2, 8, 32, 128), F32),
        V((2, 4, 10, 32, 128), F32), V((2, 2, 2, 8, 128), F32), V((2, 2, 2, 8, 128), F32),
        V((2, 4, 10, 32, 128), F32), V((2, 2, 2, 8, 128), F32), V((2, 2, 2, 8, 128), F32),
        V((8, 8, 128), F32), V((8, 64, 128), F32), V((8, 128, 128), BF16), V((8, 128), F32), V((8, 128), F32),
        V((16, 8, 128), F32), V((8, 128), F32), V((2, 8, 128), F32),
        V((8, 32, 128), F32), V((8, 32, 128), F32), V((8, 32, 128), F32), V((16, 16, 128), F32), V((16, 128), F32),
        V((3, 2, 128, 128), BF16), V((3, 2, 128, 128), F32), V((4, 16), jnp.int32), V((2, 2), jnp.int32),
        V((2, 2, 64), jnp.int32), V((2, 64), F32), V((2, 8, 128), F32),
        D((5, 4)), D((5, 2)), D((5, 2)), D((2, 4)), D((2, 4)), D((3, 2, 4)), D((3,)), D((4, 2)), D((4, 2)), D, D,
        D((2, 4)), D((2, 4)), D((2, 4)), D((2, 4)), D((16,)), D, D((2,)), D, D((8,)), D((8,)), D((16,)), D, D((16,)), D,
        D((5,)),
    ]
    gradient, readings = pl.pallas_call(
        kernel,
        out_shape=(jax.ShapeDtypeStruct((2, 128, 128), F32), jax.ShapeDtypeStruct((2, 64), F32)),
        in_specs=[pl.BlockSpec(memory_space=pl.ANY)] * 9,
        out_specs=(pl.BlockSpec(memory_space=pltpu.VMEM), pl.BlockSpec(memory_space=pltpu.VMEM)),
        scratch_shapes=scratch,
        compiler_params=pltpu.CompilerParams(collective_id=0, has_side_effects=True),
        name="survey_gradient",
    )(
        concentration, velocity, porosity, contacts.T, sources, jnp.swapaxes(receivers, 1, 2), observed,
        potential_init, adjoint_init,
    )
    return gradient, readings


def solution(mesh):
    return jax.shard_map(
        on_device,
        mesh=mesh,
        in_specs=(
            P("space", None, None),
            P(None, "space", None, None),
            P("space", None, None),
            P("space", None),
            P("tm", None),
            P("tm", None, None),
            P("tm", None),
            P("tm", "space", None, None),
            P("tm", "space", None, None),
        ),
        out_specs=(P("space", None, None), P("tm", None)),
        check_vma=False,
    )
```

```python
import jax
import jax.numpy as jnp
from jax import lax
from jax.experimental import pallas as pl
from jax.experimental.pallas import tpu as pltpu
from jax.sharding import PartitionSpec as P

STEPS = 8
RELAX_SWEEPS = 6
MESH = pl.DeviceIdType.MESH
F32 = jnp.float32
BF16 = jnp.bfloat16


def harmonic(first, second):
    return 2.0 * (first * second) / (first + second)


def iota(shape, dim):
    return lax.broadcasted_iota(jnp.int32, shape, dim)


def parts(a):
    high = a.astype(BF16)
    rest = a - high.astype(F32)
    middle = rest.astype(BF16)
    low = (rest - middle.astype(F32)).astype(BF16)
    return jnp.concatenate([high, middle, low], axis=0)


def total(product):
    rows = product.shape[0] // 3
    return product[:rows] + (product[rows : 2 * rows] + product[2 * rows :])


def dot(a, exact):
    dims = (((1,), (0,)), ((), ()))
    return total(lax.dot_general(parts(a), exact.astype(BF16), dims, preferred_element_type=F32))


def dot_t(a, exact):
    dims = (((1,), (1,)), ((), ()))
    return total(lax.dot_general(parts(a), exact.astype(BF16), dims, preferred_element_type=F32))


def kernel(
    conc, vel, poro, contacts, sources, receivers, observed, pot, adj, grad, read,
    ct, yct, yst, tv, sg, ysg, yss, coef, rdiag, bsrc,
    pf, ypf, ypsend, af, yaf, yasend,
    mbuf, rt, lt, vb, vsend, vall, rsend, rdin,
    gbuf, grx, gsum, rsbuf, osum, vbf, vf, cin, sin, rin, oin, msend,
    in_s, out_s, in_r, rel_s, t_s, t_r, sw_s, sw_r, sg_s, sg_r, tile_s, tile_r,
    p_s, p_r, a_s, a_r, v_s, v_r, rd_s, rd_r, gx_s, gx_r, rs_s, rs_r, ag_s, ag_r, fetch,
):
    space = lax.axis_index("space")
    tm = lax.axis_index("tm")
    zh = space // 16
    x = (space // 4) % 4
    y = space % 4
    zl = tm // 2
    c = tm % 2
    z = zh * 8 + zl

    def dev(x_, y_, z_, c_):
        return {"space": (z_ // 8) * 16 + x_ * 4 + y_, "tm": (z_ % 8) * 2 + c_}

    def remote(src, dst, s, r, where):
        return pltpu.make_async_remote_copy(
            src_ref=src, dst_ref=dst, send_sem=s, recv_sem=r, device_id=where, device_id_type=MESH
        )

    def arrived(ref, sem):
        pltpu.make_async_copy(ref, ref, sem).wait()

    def start_y(copies):
        @pl.when(y < 3)
        def _():
            copies[0].start()

        @pl.when(y > 0)
        def _():
            copies[1].start()

    def wait_y(copies):
        @pl.when(y < 3)
        def _():
            copies[0].wait_send()
            copies[1].wait_recv()

        @pl.when(y > 0)
        def _():
            copies[1].wait_send()
            copies[0].wait_recv()

    xn = (x + 1) % 4
    xp = (x + 3) % 4
    yn = (y + 1) % 4
    yp = (y + 3) % 4
    x_last = (x + 1) // 4
    x_first = (3 - x) // 3

    zero_plane = jnp.zeros((32, 128), F32)

    @pl.when((x == 0) & (c == 0))
    def _():
        for par in range(2):
            ct[par, 0] = zero_plane

    @pl.when((x == 3) & (c == 1))
    def _():
        for par in range(2):
            ct[par, 9] = zero_plane

    @pl.when(x == 0)
    def _():
        sg[1, 0] = zero_plane
        for f in (pf, af):
            for par in range(2):
                f[par, 1, 0] = zero_plane

    @pl.when(x == 3)
    def _():
        sg[2, 9] = zero_plane
        for f in (pf, af):
            for par in range(2):
                f[par, 2, 9] = zero_plane

    for d in range(2):
        @pl.when(y == 3 * d)
        def _():
            ysg[d, 0] = jnp.zeros((2, 8, 128), F32)
            for yf in (ypf, yaf):
                for par in range(2):
                    yf[par, d] = jnp.zeros((2, 8, 128), F32)
            for par in range(2):
                yct[par, d, 0] = jnp.zeros((8, 128), F32)

    barrier = pltpu.get_barrier_semaphore()

    def greet(where):
        pl.semaphore_signal(barrier, inc=1, device_id=where, device_id_type=MESH)

    def greet_row(k, carry):
        greet(dev(x, (y + k // 2) % 4, z, (c + k % 2) % 2))
        return carry

    def greet_plane(k, carry):
        greet(dev((x + 1 + k // 8) % 4, (k // 2) % 4, z, k % 2))
        return carry

    def greet_column(k, carry):
        greet(dev(x, y, (z + 1 + k // 2) % 16, k % 2))
        greet(dev(x, y, (z + 15 - k // 2) % 16, k % 2))
        return carry

    def greet_far(k, carry):
        greet(dev(x, (y + k) % 4, (z + 4) % 16, c))
        greet(dev(x, (y + k) % 4, (z + 12) % 16, c))
        greet(dev(x, (y + k) % 4, (z + 1) % 16, c))
        greet(dev(x, (y + k) % 4, (z + 15) % 16, c))
        return carry

    lax.fori_loop(0, 8, greet_column, 0)
    lax.fori_loop(1, 4, greet_far, 0)
    lax.fori_loop(1, 8, greet_row, 0)
    lax.fori_loop(0, 24, greet_plane, 0)

    fetched = [
        pltpu.make_async_copy(a, b, fetch.at[k])
        for k, (a, b) in enumerate(((vel, vbf), (contacts, cin), (sources, sin), (receivers, rin), (observed, oin)))
    ]
    for copy in fetched:
        copy.start()
    for copy in fetched:
        copy.wait()
    for d in range(3):
        for p in range(2):
            vf[d, p] = vbf[d, p].astype(F32)
    cells = cin[...]
    msend[...] = jnp.zeros((2, 8, 128), F32)
    for j in range(2):
        msend[j, 0:4, :] = jnp.full((4, 128), -1.0, F32)
        for k in range(4):
            msend[j, 0:1, 16 * k : 16 * k + 16] = (cells[k : k + 1] // 128).astype(F32)
            msend[j, 1:2, 16 * k : 16 * k + 16] = (cells[k : k + 1] % 128).astype(F32)
        for k in range(2):
            msend[j, 2 + k : 3 + k, 0:64] = rin[j, k : k + 1, :].astype(F32)
            msend[j, 5 + k : 6 + k, :] = jnp.broadcast_to(sin[j : j + 1, k : k + 1].astype(F32), (1, 128))
        msend[j, 4:5, 0:64] = oin[j : j + 1, :]
    pl.semaphore_wait(barrier, 16 + 12 + 7 + 24)

    zz = (z + 8 * c) % 16
    home = zz < 8

    def swap_copy(which, j, d):
        up4 = (j + zh + 1) % 2
        zt4 = (z + 4 * up4 + 12 * (1 - up4)) % 16
        yt = (y + d) % 4
        where = dev(x, yt, zt4, c)
        if which == 2:
            return remote(msend.at[j], mbuf.at[zh * 4 + y], sw_s.at[2, j, d], sw_r.at[2], where)
        src = (pot, adj)[which].at[j, :, pl.ds(pl.multiple_of(32 * yt, 32), 32)]
        dst = (pf, af)[which].at[0, 1 + zh, pl.ds(1 + 2 * y, 2)]
        return remote(src, dst, sw_s.at[which, j, d], sw_r.at[which], where)

    def swap_copies(which, j):
        return [swap_copy(which, j, d) for d in range(4)]

    def landing(a, g):
        return ct.at[0, pl.ds(1 + 4 * g, 4)] if a == 0 else tv.at[a - 1, pl.ds(4 * g, 4)]

    def landing_two(a):
        return ct.at[0, pl.ds(1 + 2 * y, 2)] if a == 0 else tv.at[a - 1, pl.ds(2 * y, 2)]

    def in_rows(a, yt):
        rows = pl.ds(pl.multiple_of(32 * yt, 32), 32)
        return conc.at[:, rows] if a == 0 else poro.at[:, rows] if a == 4 else vf.at[a - 1, :, rows]

    def in_copy(a, d):
        yt = (y + d) % 4
        return remote(in_rows(a, yt), landing_two(a), in_s.at[a, d], in_r.at[a, y // 2], dev(x, yt, z, c))

    up = jnp.where((zz >= 7) & (zz <= 10), 1, 0)
    down = jnp.where((zz == 0) | (zz >= 13), 1, 0)
    zt = (z + up + 15 * down) % 16
    passing = (up + down > 0) & (zz >= 8)
    leaving = (zz == 7) | (zz == 0)

    def out_copy(a, d):
        yt = (y + d) % 4
        return remote(in_rows(a, yt), landing_two(a), out_s.at[a, d], in_r.at[a, y // 2], dev(x, yt, zt, c))

    def in_local(a):
        return pltpu.make_async_copy(in_rows(a, y), landing_two(a), in_r.at[a, y // 2])

    @pl.when(home)
    def _():
        for a in range(5):
            @pl.when(leaving)
            def _():
                for d in range(4):
                    out_copy(a, d).start()

            for d in range(1, 4):
                in_copy(a, d).start()
            in_local(a).start()

    for j in range(2):
        for copy in swap_copies(2, j):
            copy.start()
    def relay(a, g):
        return remote(landing(a, g), landing(a, g), rel_s.at[a, g], in_r.at[a, g], dev(x, y, zt, c))

    def pass_on(a):
        for g in range(2):
            arrived(landing(a, g), in_r.at[a, g])

            @pl.when(passing)
            def _():
                relay(a, g).start()

    def passed_on(arrays):
        @pl.when(passing)
        def _():
            for a in arrays:
                for g in range(2):
                    relay(a, g).wait_send()

    def t_x(par):
        return [
            remote(ct.at[par, 8], ct.at[par, 10 * x_last * c], t_s.at[par, 0], t_r.at[par, 0],
                   dev(xn, y, z, (c + x_last) % 2)),
            remote(ct.at[par, 1], ct.at[par, 9 + 2 * x_first * (1 - c)], t_s.at[par, 1], t_r.at[par, 1],
                   dev(xp, y, z, (c + x_first) % 2)),
        ]

    def t_y(par):
        return [
            remote(yst.at[par, 0], yct.at[par, 0, 0], t_s.at[par, 2], t_r.at[par, 2], dev(x, yn, z, c)),
            remote(yst.at[par, 1], yct.at[par, 1, 0], t_s.at[par, 3], t_r.at[par, 3], dev(x, yp, z, c)),
        ]

    row = iota((32, 128), 0)
    lane = iota((32, 128), 1)

    def shift_y(v, low, high):
        below = jnp.where(row == 0, low, pltpu.roll(v, 1, 0))
        above = jnp.where(row == 31, high, pltpu.roll(v, 31, 0))
        return below, above

    def t_rows(par, p, v):
        yst[par, 0, p : p + 1, :] = v[31:32]
        yst[par, 1, p : p + 1, :] = v[0:1]

    pass_on(0)
    for copy in t_x(0):
        copy.start()
    for p in range(8):
        t_rows(0, p, ct[0, p + 1])
    start_y(t_y(0))
    for j in range(2):
        for d in range(4):
            swap_copy(0, j, d).start()
    for a in range(1, 4):
        pass_on(a)
    passed_on([0])

    def t_step(par, last):
        new = 1 - par

        def plane(p):
            v = ct[par, p + 1]
            xlow = ct[par, p]
            xhigh = ct[par, p + 2]
            ylow, yhigh = shift_y(v, yct[par, 0, 0, p : p + 1, :], yct[par, 1, 0, p : p + 1, :])
            zlow = jnp.where(lane == 0, 0.0, pltpu.roll(v, 1, 1))
            zhigh = jnp.where(lane == 127, 0.0, pltpu.roll(v, 127, 1))
            change = None
            for d, (low, high) in enumerate(((xlow, xhigh), (ylow, yhigh), (zlow, zhigh))):
                speed = tv[d, p]
                term = jnp.maximum(speed, 0.0) * (v - low) + jnp.minimum(speed, 0.0) * (high - v)
                change = term if change is None else change + term
            v = v - change
            ct[new, p + 1] = v
            t_rows(new, p, v)

        wait_y(t_y(par))
        for copy in t_x(par):
            copy.wait()
        plane(0)
        plane(7)

        @pl.when(jnp.logical_not(last))
        def _():
            for copy in t_x(new):
                copy.start()

        for p in range(1, 7):
            plane(p)

        @pl.when(jnp.logical_not(last))
        def _():
            start_y(t_y(new))

    def tables(k):
        q = iota((64, 128), 0)
        target = ((q // 32) * 128 + q % 32 + 32 * y).astype(F32)
        rt[k] = jnp.where(target == mbuf[k, 0:1, :], 1.0, 0.0)
        lt[k] = jnp.where(iota((128, 128), 0).astype(F32) == mbuf[k, 1:2, :], 1.0, 0.0).astype(BF16)

    arrived(mbuf, sw_r.at[2])

    def t_two(s, carry):
        t_step(0, s < 0)
        tables(2 * s)

        @pl.when(s == 0)
        def _():
            pass_on(4)

        t_step(1, s == STEPS // 2 - 1)
        tables(2 * s + 1)

        return carry

    lax.fori_loop(0, STEPS // 2, t_two, 0)
    passed_on(range(1, 5))

    for p in range(8):
        v = jnp.exp(1.8 * jnp.log(tv[3, p])) * (0.5 + ct[0, p + 1])
        sg[1 + c, p + 1] = v
        yss[0, p : p + 1, :] = v[31:32]
        yss[1, p : p + 1, :] = v[0:1]

    def sg_x(cc):
        return [
            remote(sg.at[1 + c, 8], sg.at[1 + c + x_last, 0], sg_s.at[0, cc], sg_r.at[0, c], dev(xn, y, z, cc)),
            remote(sg.at[1 + c, 1], sg.at[1 + c - x_first, 9], sg_s.at[1, cc], sg_r.at[1, c], dev(xp, y, z, cc)),
        ]

    def sg_y(cc):
        return [
            remote(yss.at[0], ysg.at[0, 0, c], sg_s.at[2, cc], sg_r.at[2, c], dev(x, yn, z, cc)),
            remote(yss.at[1], ysg.at[1, 0, c], sg_s.at[3, cc], sg_r.at[3, c], dev(x, yp, z, cc)),
        ]

    tile_copy = remote(
        sg.at[1 + c, pl.ds(1, 8)], sg.at[1 + c, pl.ds(1, 8)], tile_s, tile_r, dev(x, y, z, 1 - c)
    )
    tile_copy.start()
    for cc in range(2):
        start_y(sg_y(cc))
        for copy in sg_x(cc):
            copy.start()
    for j in range(2):
        for d in range(4):
            swap_copy(1, j, d).start()

    jj = iota((128, 128), 0)
    mm = iota((128, 128), 1)
    spread = jnp.where((jj % 16 == mm % 16) & (mm < 64), 0.25, 0.0)
    own = jnp.where(iota((8, 128), 1) // 16 == iota((8, 128), 0), 1.0, 0.0)
    r0 = mbuf[0, 2:3, :]
    r1 = mbuf[0, 3:4, :]
    measured = mbuf[0, 4:5, :]
    ja = mbuf[0, 5:6, :]
    jb = mbuf[0, 6:7, :]

    def inject(current, finish):
        vals = dot(jnp.broadcast_to(current, (8, 128)) * own, spread)
        for k in range(8):
            h, pair = k // 4, 2 * (k % 4)
            block = dot_t(rt[k] * vals[k : k + 1, :], lt[k])
            for n in range(2):
                rows = block[32 * n : 32 * n + 32]
                bsrc[h, pair + n] = rows * rdiag[h, pair + n] if finish else rows

    def field(f, yf, ysend, s_sem, r_sem):
        def x_copies(par):
            return [
                remote(f.at[par, pl.ds(1, 2), 8], f.at[par, pl.ds(1 + x_last, 2), 0],
                       s_sem.at[par, 0], r_sem.at[par, 0], dev(xn, y, z, c)),
                remote(f.at[par, pl.ds(1, 2), 1], f.at[par, pl.ds(1 - x_first, 2), 9],
                       s_sem.at[par, 1], r_sem.at[par, 1], dev(xp, y, z, c)),
            ]

        def y_copies(par):
            return [
                remote(ysend.at[par, 0], yf.at[par, 0], s_sem.at[par, 2], r_sem.at[par, 2], dev(x, yn, z, c)),
                remote(ysend.at[par, 1], yf.at[par, 1], s_sem.at[par, 3], r_sem.at[par, 3], dev(x, yp, z, c)),
            ]

        def edge_rows(par, h, p, v):
            ysend[par, 0, h, p : p + 1, :] = v[31:32]
            ysend[par, 1, h, p : p + 1, :] = v[0:1]

        def begin():
            for copy in x_copies(0):
                copy.start()
            for h in range(2):
                for p in range(8):
                    edge_rows(0, h, p, f[0, 1 + h, p + 1])
            start_y(y_copies(0))

        def end(par=0):
            wait_y(y_copies(par))
            for copy in x_copies(par):
                copy.wait()

        def sweep(par):
            new = 1 - par

            def plane(h, p):
                v = f[par, 1 + h, p + 1]
                ylow, yhigh = shift_y(v, yf[par, 0, h, p : p + 1, :], yf[par, 1, h, p : p + 1, :])
                out = coef[0, h, p] * f[par, 1 + h, p + 2] + coef[1, h, p] * f[par, 1 + h, p]
                out = out + (coef[2, h, p] * yhigh + coef[3, h, p] * ylow)
                out = out + (coef[4, h, p] * pltpu.roll(v, 127, 1) + coef[5, h, p] * pltpu.roll(v, 1, 1))
                out = (0.2 * v + bsrc[h, p]) + out
                f[new, 1 + h, p + 1] = out
                edge_rows(new, h, p, out)

            end(par)
            for p in (0, 7):
                for h in range(2):
                    plane(h, p)
            for copy in x_copies(new):
                copy.start()
            for h in range(2):
                for p in range(1, 7):
                    plane(h, p)
            start_y(y_copies(new))

        def two(s, carry):
            sweep(0)
            sweep(1)
            return carry

        def sweeps():
            lax.fori_loop(0, RELAX_SWEEPS // 2, two, 0)

        return begin, sweeps, end

    own_lane = iota((1, 128), 1)
    own_ids = ((own_lane // 64) * 256 + x * 64 + own_lane % 64).astype(F32)
    inject(4.0 * (jnp.where(own_ids == ja, 1.0, 0.0) - jnp.where(own_ids == jb, 1.0, 0.0)), False)

    p_begin, p_sweeps, p_end = field(pf, ypf, ypsend, p_s, p_r)
    a_begin, a_sweeps, a_end = field(af, yaf, yasend, a_s, a_r)
    arrived(pf.at[0, pl.ds(1, 2), pl.ds(1, 8)], sw_r.at[0])
    p_begin()
    tile_copy.wait()
    for cc in range(2):
        for d, copy in enumerate(sg_x(cc)):
            copy.wait_send()
            arrived(sg.at[1, 0], sg_r.at[d, cc])

        @pl.when(y < 3)
        def _():
            sg_y(cc)[0].wait_send()
            arrived(yss.at[0], sg_r.at[3, cc])

        @pl.when(y > 0)
        def _():
            sg_y(cc)[1].wait_send()
            arrived(yss.at[0], sg_r.at[2, cc])

    def faces_of(h, p):
        s = sg[1 + h, p + 1]
        low = ysg[0, 0, h, p : p + 1, :]
        high = ysg[1, 0, h, p : p + 1, :]
        _, syp = shift_y(s, low, high)
        szp = jnp.where(lane == 127, 0.0, pltpu.roll(s, 127, 1))
        ux = harmonic(s, sg[1 + h, p + 2])
        uy = harmonic(s, syp)
        uz = harmonic(s, szp)
        return s, low, ux, uy, uz

    for h in range(2):
        lx = harmonic(sg[1 + h, 0], sg[1 + h, 1])
        for p in range(8):
            s, low, ux, uy, uz = faces_of(h, p)
            ly = jnp.where(row == 0, harmonic(low, s[0:1]), pltpu.roll(uy, 1, 0))
            lz = pltpu.roll(uz, 1, 1)
            r = 0.8 / (ux + lx + uy + ly + uz + lz)
            rdiag[h, p] = r
            bsrc[h, p] = bsrc[h, p] * r
            for k, face in enumerate((ux, lx, uy, ly, uz, lz)):
                coef[k, h, p] = face * r
            lx = ux

    def electrode_ids(x_):
        j = iota((128, 128), 0)
        return ((j // 64) * 256 + x_ * 64 + j % 64).astype(F32)

    p_sweeps()

    for k in range(8):
        h, pair = k // 4, 2 * (k % 4)
        block = pf[0, 1 + h, pl.ds(1 + pair, 2)].reshape(64, 128)
        vb[k : k + 1, :] = jnp.sum(rt[k] * dot(block, lt[k]), axis=0, keepdims=True)
    part = jnp.sum(dot_t(vb[...], spread) * own, axis=0, keepdims=True)
    vsend[...] = jnp.broadcast_to(part, (8, 128))

    def v_copy(k):
        xt = (x + k // 4) % 4
        yt = (y + k % 4) % 4
        return remote(vsend, vall.at[x * 4 + y], v_s.at[k], v_r, dev(xt, yt, z, c))

    for k in range(1, 16):
        v_copy(k).start()
    pltpu.make_async_copy(vsend, vall.at[x * 4 + y], v_r).start()
    arrived(af.at[0, pl.ds(1, 2), pl.ds(1, 8)], sw_r.at[1])
    a_begin()
    arrived(vall, v_r)

    def selector(x_):
        ids = electrode_ids(x_)
        return jnp.where(ids == r0, 1.0, 0.0) - jnp.where(ids == r1, 1.0, 0.0)

    readings = jnp.zeros((8, 128), F32)
    for k in range(4):
        volts = vall[4 * k] + vall[4 * k + 1] + vall[4 * k + 2] + vall[4 * k + 3]
        readings = readings + dot(volts, selector(k))
    rsend[...] = readings
    survey = (1 + zh + zl // 4) % 2

    def read_copies():
        return [
            remote(rsend, rdin.at[survey], rd_s.at[half], rd_r, dev(x, y, half * 8 + (zl + 4) % 8, c))
            for half in range(2)
        ]

    for copy in read_copies():
        copy.start()
    inject(dot_t(readings - measured, selector(x))[0:1], True)
    a_sweeps()
    p_end()
    a_end()

    def terms(h, p):
        _, _, ux, uy, uz = faces_of(h, p)
        pv = pf[0, 1 + h, p + 1]
        av = af[0, 1 + h, p + 1]
        _, py = shift_y(pv, pv[0:1], ypf[0, 1, h, p : p + 1, :])
        _, ay = shift_y(av, av[0:1], yaf[0, 1, h, p : p + 1, :])
        out = ux * (pf[0, 1 + h, p + 2] - pv) * (af[0, 1 + h, p + 2] - av)
        out = out + uy * (py - pv) * (ay - av)
        out = out + uz * (pltpu.roll(pv, 127, 1) - pv) * (pltpu.roll(av, 127, 1) - av)
        return -out

    def other(p):
        return remote(gbuf.at[p], grx.at[p], gx_s.at[p], gx_r.at[p], dev(x, y, z, 1 - c))

    def rs_copy(k, local):
        p, rh = k // 2, k % 2
        src = gsum.at[p, pl.ds(16 * rh, 16)]
        dst = rsbuf.at[z]
        if local:
            return pltpu.make_async_copy(src, dst, rs_r)
        return remote(src, dst, rs_s.at[k], rs_r, dev(x, y, 8 * c + p, rh))

    def rs_self(k):
        return (z == 8 * c + k // 2) & (c == k % 2)

    for p in range(8):
        gbuf[p] = terms(1 - c, p)
        other(p).start()
    for p in range(8):
        mine = terms(c, p)
        other(p).wait()
        gsum[p] = mine + grx[p]
        for k in (2 * p, 2 * p + 1):
            @pl.when(jnp.logical_not(rs_self(k)))
            def _():
                rs_copy(k, False).start()

            @pl.when(rs_self(k))
            def _():
                rs_copy(k, True).start()

    arrived(rsbuf, rs_r)
    added = rsbuf[0]
    for k in range(1, 16):
        added = added + rsbuf[k]
    osum[...] = added

    def ag_copy(k, local):
        dst = grad.at[zl % 2, pl.ds(pl.multiple_of(32 * y + 16 * c, 16), 16)]
        if local:
            return pltpu.make_async_copy(osum, dst, ag_r)
        return remote(osum, dst, ag_s.at[k], ag_r, dev(x, zl // 2, 8 * zh + ag_z(k), k % 2))

    def ag_z(k):
        return (k // 2) * (zl // 4) + (7 - k // 2) * (1 - zl // 4)

    def ag_self(k):
        return (y == zl // 2) & (zl == ag_z(k)) & (c == k % 2)

    for k in range(16):
        @pl.when(jnp.logical_not(ag_self(k)))
        def _():
            ag_copy(k, False).start()

        @pl.when(ag_self(k))
        def _():
            ag_copy(k, True).start()

    arrived(rdin, rd_r)
    read[0:1, :] = rdin[0, 0:1, 0:64]
    read[1:2, :] = rdin[1, 0:1, 0:64]
    arrived(grad, ag_r)

    @pl.when(home)
    def _():
        for a in range(5):
            for d in range(1, 4):
                in_copy(a, d).wait_send()

            @pl.when(leaving)
            def _():
                for d in range(4):
                    out_copy(a, d).wait_send()


    for which in range(3):
        for j in range(2):
            for copy in swap_copies(which, j):
                copy.wait_send()
    for k in range(1, 16):
        v_copy(k).wait_send()
    for copy in read_copies():
        copy.wait_send()
    for k in range(16):
        @pl.when(jnp.logical_not(rs_self(k)))
        def _():
            rs_copy(k, False).wait_send()

        @pl.when(jnp.logical_not(ag_self(k)))
        def _():
            ag_copy(k, False).wait_send()


def on_device(
    concentration, velocity, porosity, contacts, sources, receivers, observed, potential_init, adjoint_init
):
    V = pltpu.VMEM
    D = pltpu.SemaphoreType.DMA
    scratch = [
        V((2, 12, 32, 128), F32), V((2, 2, 2, 8, 128), F32), V((2, 2, 8, 128), F32), V((4, 8, 32, 128), F32),
        V((4, 10, 32, 128), F32), V((2, 2, 2, 8, 128), F32), V((2, 8, 128), F32),
        V((6, 2, 8, 32, 128), F32), V((2, 8, 32, 128), F32), V((2, 8, 32, 128), F32),
        V((2, 4, 10, 32, 128), F32), V((2, 2, 2, 8, 128), F32), V((2, 2, 2, 8, 128), F32),
        V((2, 4, 10, 32, 128), F32), V((2, 2, 2, 8, 128), F32), V((2, 2, 2, 8, 128), F32),
        V((8, 8, 128), F32), V((8, 64, 128), F32), V((8, 128, 128), BF16), V((8, 128), F32), V((8, 128), F32),
        V((16, 8, 128), F32), V((8, 128), F32), V((2, 8, 128), F32),
        V((8, 32, 128), F32), V((8, 32, 128), F32), V((8, 32, 128), F32), V((16, 16, 128), F32), V((16, 128), F32),
        V((3, 2, 128, 128), BF16), V((3, 2, 128, 128), F32), V((4, 16), jnp.int32), V((2, 2), jnp.int32),
        V((2, 2, 64), jnp.int32), V((2, 64), F32), V((2, 8, 128), F32),
        D((5, 4)), D((5, 4)), D((5, 2)), D((5, 2)), D((2, 4)), D((2, 4)), D((3, 2, 4)), D((3,)), D((4, 2)), D((4, 2)), D, D,
        D((2, 4)), D((2, 4)), D((2, 4)), D((2, 4)), D((16,)), D, D((2,)), D, D((8,)), D((8,)), D((16,)), D, D((16,)), D,
        D((5,)),
    ]
    gradient, readings = pl.pallas_call(
        kernel,
        out_shape=(jax.ShapeDtypeStruct((2, 128, 128), F32), jax.ShapeDtypeStruct((2, 64), F32)),
        in_specs=[pl.BlockSpec(memory_space=pl.ANY)] * 9,
        out_specs=(pl.BlockSpec(memory_space=pltpu.VMEM), pl.BlockSpec(memory_space=pltpu.VMEM)),
        scratch_shapes=scratch,
        compiler_params=pltpu.CompilerParams(collective_id=0, has_side_effects=True),
        name="survey_gradient",
    )(
        concentration, velocity, porosity, contacts.T, sources, jnp.swapaxes(receivers, 1, 2), observed,
        potential_init, adjoint_init,
    )
    return gradient, readings


def solution(mesh):
    return jax.shard_map(
        on_device,
        mesh=mesh,
        in_specs=(
            P("space", None, None),
            P(None, "space", None, None),
            P("space", None, None),
            P("space", None),
            P("tm", None),
            P("tm", None, None),
            P("tm", None),
            P("tm", "space", None, None),
            P("tm", "space", None, None),
        ),
        out_specs=(P("space", None, None), P("tm", None)),
        check_vma=False,
    )
```

```python
import jax
import jax.numpy as jnp
from jax import lax
from jax.experimental import pallas as pl
from jax.experimental.pallas import tpu as pltpu
from jax.sharding import PartitionSpec as P

STEPS = 8
RELAX_SWEEPS = 6
MESH = pl.DeviceIdType.MESH
F32 = jnp.float32
BF16 = jnp.bfloat16


def harmonic(first, second):
    return 2.0 * (first * second) / (first + second)


def iota(shape, dim):
    return lax.broadcasted_iota(jnp.int32, shape, dim)


def parts(a):
    high = a.astype(BF16)
    rest = a - high.astype(F32)
    middle = rest.astype(BF16)
    low = (rest - middle.astype(F32)).astype(BF16)
    return jnp.concatenate([high, middle, low], axis=0)


def total(product):
    rows = product.shape[0] // 3
    return product[:rows] + (product[rows : 2 * rows] + product[2 * rows :])


def dot(a, exact):
    dims = (((1,), (0,)), ((), ()))
    return total(lax.dot_general(parts(a), exact.astype(BF16), dims, preferred_element_type=F32))


def dot_t(a, exact):
    dims = (((1,), (1,)), ((), ()))
    return total(lax.dot_general(parts(a), exact.astype(BF16), dims, preferred_element_type=F32))


def kernel(
    conc, vel, poro, contacts, sources, receivers, observed, pot, adj, grad, read,
    ct, yct, yst, tv, sg, ysg, yss, coef, rdiag, bsrc,
    pf, ypf, ypsend, af, yaf, yasend,
    mbuf, rt, lt, vb, vsend, vall, rsend, rdin,
    gbuf, grx, gsum, rsbuf, osum, vbf, vf, cin, sin, rin, oin, msend,
    in_s, out_s, in_r, rel_s, t_s, t_r, sw_s, sw_r, sg_s, sg_r, tile_s, tile_r,
    p_s, p_r, a_s, a_r, v_s, v_r, rd_s, rd_r, gx_s, gx_r, rs_s, rs_r, ag_s, ag_r, fetch,
):
    space = lax.axis_index("space")
    tm = lax.axis_index("tm")
    zh = space // 16
    x = (space // 4) % 4
    y = space % 4
    zl = tm // 2
    c = tm % 2
    z = zh * 8 + zl

    def dev(x_, y_, z_, c_):
        return {"space": (z_ // 8) * 16 + x_ * 4 + y_, "tm": (z_ % 8) * 2 + c_}

    def remote(src, dst, s, r, where):
        return pltpu.make_async_remote_copy(
            src_ref=src, dst_ref=dst, send_sem=s, recv_sem=r, device_id=where, device_id_type=MESH
        )

    def arrived(ref, sem):
        pltpu.make_async_copy(ref, ref, sem).wait()

    def start_y(copies):
        @pl.when(y < 3)
        def _():
            copies[0].start()

        @pl.when(y > 0)
        def _():
            copies[1].start()

    def wait_y(copies):
        @pl.when(y < 3)
        def _():
            copies[0].wait_send()
            copies[1].wait_recv()

        @pl.when(y > 0)
        def _():
            copies[1].wait_send()
            copies[0].wait_recv()

    xn = (x + 1) % 4
    xp = (x + 3) % 4
    yn = (y + 1) % 4
    yp = (y + 3) % 4
    x_last = (x + 1) // 4
    x_first = (3 - x) // 3

    zero_plane = jnp.zeros((32, 128), F32)

    @pl.when((x == 0) & (c == 0))
    def _():
        for par in range(2):
            ct[par, 0] = zero_plane

    @pl.when((x == 3) & (c == 1))
    def _():
        for par in range(2):
            ct[par, 9] = zero_plane

    @pl.when(x == 0)
    def _():
        sg[1, 0] = zero_plane
        for f in (pf, af):
            for par in range(2):
                f[par, 1, 0] = zero_plane

    @pl.when(x == 3)
    def _():
        sg[2, 9] = zero_plane
        for f in (pf, af):
            for par in range(2):
                f[par, 2, 9] = zero_plane

    for d in range(2):
        @pl.when(y == 3 * d)
        def _():
            ysg[d, 0] = jnp.zeros((2, 8, 128), F32)
            for yf in (ypf, yaf):
                for par in range(2):
                    yf[par, d] = jnp.zeros((2, 8, 128), F32)
            for par in range(2):
                yct[par, d, 0] = jnp.zeros((8, 128), F32)

    barrier = pltpu.get_barrier_semaphore()

    def greet(where):
        pl.semaphore_signal(barrier, inc=1, device_id=where, device_id_type=MESH)

    def greet_row(k, carry):
        greet(dev(x, (y + k // 2) % 4, z, (c + k % 2) % 2))
        return carry

    def greet_plane(k, carry):
        greet(dev((x + 1 + k // 8) % 4, (k // 2) % 4, z, k % 2))
        return carry

    def greet_column(k, carry):
        greet(dev(x, y, (z + 1 + k // 2) % 16, k % 2))
        greet(dev(x, y, (z + 15 - k // 2) % 16, k % 2))
        return carry

    def greet_far(k, carry):
        greet(dev(x, (y + k) % 4, (z + 4) % 16, c))
        greet(dev(x, (y + k) % 4, (z + 12) % 16, c))
        greet(dev(x, (y + k) % 4, (z + 1) % 16, c))
        greet(dev(x, (y + k) % 4, (z + 15) % 16, c))
        return carry

    lax.fori_loop(0, 8, greet_column, 0)
    lax.fori_loop(1, 4, greet_far, 0)
    lax.fori_loop(1, 8, greet_row, 0)
    lax.fori_loop(0, 24, greet_plane, 0)

    fetched = [
        pltpu.make_async_copy(a, b, fetch.at[k])
        for k, (a, b) in enumerate(((vel, vbf), (contacts, cin), (sources, sin), (receivers, rin), (observed, oin)))
    ]
    for copy in fetched:
        copy.start()
    for copy in fetched:
        copy.wait()
    for d in range(3):
        for p in range(2):
            vf[d, p] = vbf[d, p].astype(F32)
    cells = cin[...]
    msend[...] = jnp.zeros((2, 8, 128), F32)
    for j in range(2):
        msend[j, 0:4, :] = jnp.full((4, 128), -1.0, F32)
        for k in range(4):
            msend[j, 0:1, 16 * k : 16 * k + 16] = (cells[k : k + 1] // 128).astype(F32)
            msend[j, 1:2, 16 * k : 16 * k + 16] = (cells[k : k + 1] % 128).astype(F32)
        for k in range(2):
            msend[j, 2 + k : 3 + k, 0:64] = rin[j, k : k + 1, :].astype(F32)
            msend[j, 5 + k : 6 + k, :] = jnp.broadcast_to(sin[j : j + 1, k : k + 1].astype(F32), (1, 128))
        msend[j, 4:5, 0:64] = oin[j : j + 1, :]
    pl.semaphore_wait(barrier, 16 + 12 + 7 + 24)

    zz = (z + 8 * c) % 16
    home = zz < 8

    def swap_copy(which, j, d):
        up4 = (j + zh + 1) % 2
        zt4 = (z + 4 * up4 + 12 * (1 - up4)) % 16
        yt = (y + d) % 4
        where = dev(x, yt, zt4, c)
        if which == 2:
            return remote(msend.at[j], mbuf.at[zh * 4 + y], sw_s.at[2, j, d], sw_r.at[2], where)
        src = (pot, adj)[which].at[j, :, pl.ds(pl.multiple_of(32 * yt, 32), 32)]
        dst = (pf, af)[which].at[0, 1 + zh, pl.ds(1 + 2 * y, 2)]
        return remote(src, dst, sw_s.at[which, j, d], sw_r.at[which], where)

    def swap_copies(which, j):
        return [swap_copy(which, j, d) for d in range(4)]

    def landing(a, g):
        return ct.at[0, pl.ds(1 + 4 * g, 4)] if a == 0 else tv.at[a - 1, pl.ds(4 * g, 4)]

    def landing_two(a):
        return ct.at[0, pl.ds(1 + 2 * y, 2)] if a == 0 else tv.at[a - 1, pl.ds(2 * y, 2)]

    def in_rows(a, yt):
        rows = pl.ds(pl.multiple_of(32 * yt, 32), 32)
        return conc.at[:, rows] if a == 0 else poro.at[:, rows] if a == 4 else vf.at[a - 1, :, rows]

    def in_copy(a, d):
        yt = (y + d) % 4
        return remote(in_rows(a, yt), landing_two(a), in_s.at[a, d], in_r.at[a, y // 2], dev(x, yt, z, c))

    up = jnp.where((zz >= 7) & (zz <= 10), 1, 0)
    down = jnp.where((zz == 0) | (zz >= 13), 1, 0)
    zt = (z + up + 15 * down) % 16
    passing = (up + down > 0) & (zz >= 8)
    leaving = (zz == 7) | (zz == 0)

    def out_copy(a, d):
        yt = (y + d) % 4
        return remote(in_rows(a, yt), landing_two(a), out_s.at[a, d], in_r.at[a, y // 2], dev(x, yt, zt, c))

    def in_local(a):
        return pltpu.make_async_copy(in_rows(a, y), landing_two(a), in_r.at[a, y // 2])

    @pl.when(home)
    def _():
        for a in range(5):
            @pl.when(leaving)
            def _():
                for d in range(4):
                    out_copy(a, d).start()

            for d in range(1, 4):
                in_copy(a, d).start()
            in_local(a).start()

    for j in range(2):
        for copy in swap_copies(2, j):
            copy.start()
    def relay(a, g):
        return remote(landing(a, g), landing(a, g), rel_s.at[a, g], in_r.at[a, g], dev(x, y, zt, c))

    def pass_on(a):
        for g in range(2):
            arrived(landing(a, g), in_r.at[a, g])

            @pl.when(passing)
            def _():
                relay(a, g).start()

    def passed_on(arrays):
        @pl.when(passing)
        def _():
            for a in arrays:
                for g in range(2):
                    relay(a, g).wait_send()

    def t_x(par):
        return [
            remote(ct.at[par, 8], ct.at[par, 10 * x_last * c], t_s.at[par, 0], t_r.at[par, 0],
                   dev(xn, y, z, (c + x_last) % 2)),
            remote(ct.at[par, 1], ct.at[par, 9 + 2 * x_first * (1 - c)], t_s.at[par, 1], t_r.at[par, 1],
                   dev(xp, y, z, (c + x_first) % 2)),
        ]

    def t_y(par):
        return [
            remote(yst.at[par, 0], yct.at[par, 0, 0], t_s.at[par, 2], t_r.at[par, 2], dev(x, yn, z, c)),
            remote(yst.at[par, 1], yct.at[par, 1, 0], t_s.at[par, 3], t_r.at[par, 3], dev(x, yp, z, c)),
        ]

    row = iota((32, 128), 0)
    lane = iota((32, 128), 1)

    def shift_y(v, low, high):
        below = jnp.where(row == 0, low, pltpu.roll(v, 1, 0))
        above = jnp.where(row == 31, high, pltpu.roll(v, 31, 0))
        return below, above

    def t_rows(par, p, v):
        yst[par, 0, p : p + 1, :] = v[31:32]
        yst[par, 1, p : p + 1, :] = v[0:1]

    pass_on(0)
    for copy in t_x(0):
        copy.start()
    for p in range(8):
        t_rows(0, p, ct[0, p + 1])
    start_y(t_y(0))
    for d in range(4):
        for j in range(2):
            swap_copy(0, j, d).start()
    for a in range(1, 4):
        pass_on(a)
    passed_on([0])

    def t_step(par, last):
        new = 1 - par

        def plane(p):
            v = ct[par, p + 1]
            xlow = ct[par, p]
            xhigh = ct[par, p + 2]
            ylow, yhigh = shift_y(v, yct[par, 0, 0, p : p + 1, :], yct[par, 1, 0, p : p + 1, :])
            zlow = jnp.where(lane == 0, 0.0, pltpu.roll(v, 1, 1))
            zhigh = jnp.where(lane == 127, 0.0, pltpu.roll(v, 127, 1))
            change = None
            for d, (low, high) in enumerate(((xlow, xhigh), (ylow, yhigh), (zlow, zhigh))):
                speed = tv[d, p]
                term = jnp.maximum(speed, 0.0) * (v - low) + jnp.minimum(speed, 0.0) * (high - v)
                change = term if change is None else change + term
            v = v - change
            ct[new, p + 1] = v
            t_rows(new, p, v)

        wait_y(t_y(par))
        for copy in t_x(par):
            copy.wait()
        plane(0)
        plane(7)

        @pl.when(jnp.logical_not(last))
        def _():
            for copy in t_x(new):
                copy.start()

        for p in range(1, 7):
            plane(p)

        @pl.when(jnp.logical_not(last))
        def _():
            start_y(t_y(new))

    def tables(k):
        q = iota((64, 128), 0)
        target = ((q // 32) * 128 + q % 32 + 32 * y).astype(F32)
        rt[k] = jnp.where(target == mbuf[k, 0:1, :], 1.0, 0.0)
        lt[k] = jnp.where(iota((128, 128), 0).astype(F32) == mbuf[k, 1:2, :], 1.0, 0.0).astype(BF16)

    arrived(mbuf, sw_r.at[2])

    def t_two(s, carry):
        t_step(0, s < 0)
        tables(2 * s)

        @pl.when((s == 0) & passing)
        def _():
            pass_on(4)

        t_step(1, s == STEPS // 2 - 1)
        tables(2 * s + 1)

        return carry

    lax.fori_loop(0, STEPS // 2, t_two, 0)

    @pl.when(jnp.logical_not(passing))
    def _():
        for g in range(2):
            arrived(landing(4, g), in_r.at[4, g])

    passed_on(range(1, 5))

    for p in range(8):
        v = jnp.exp(1.8 * jnp.log(tv[3, p])) * (0.5 + ct[0, p + 1])
        sg[1 + c, p + 1] = v
        yss[0, p : p + 1, :] = v[31:32]
        yss[1, p : p + 1, :] = v[0:1]

    def sg_x(cc):
        return [
            remote(sg.at[1 + c, 8], sg.at[1 + c + x_last, 0], sg_s.at[0, cc], sg_r.at[0, c], dev(xn, y, z, cc)),
            remote(sg.at[1 + c, 1], sg.at[1 + c - x_first, 9], sg_s.at[1, cc], sg_r.at[1, c], dev(xp, y, z, cc)),
        ]

    def sg_y(cc):
        return [
            remote(yss.at[0], ysg.at[0, 0, c], sg_s.at[2, cc], sg_r.at[2, c], dev(x, yn, z, cc)),
            remote(yss.at[1], ysg.at[1, 0, c], sg_s.at[3, cc], sg_r.at[3, c], dev(x, yp, z, cc)),
        ]

    tile_copy = remote(
        sg.at[1 + c, pl.ds(1, 8)], sg.at[1 + c, pl.ds(1, 8)], tile_s, tile_r, dev(x, y, z, 1 - c)
    )
    tile_copy.start()
    for cc in range(2):
        start_y(sg_y(cc))
        for copy in sg_x(cc):
            copy.start()
    for d in range(4):
        for j in range(2):
            swap_copy(1, j, d).start()

    jj = iota((128, 128), 0)
    mm = iota((128, 128), 1)
    spread = jnp.where((jj % 16 == mm % 16) & (mm < 64), 0.25, 0.0)
    own = jnp.where(iota((8, 128), 1) // 16 == iota((8, 128), 0), 1.0, 0.0)
    r0 = mbuf[0, 2:3, :]
    r1 = mbuf[0, 3:4, :]
    measured = mbuf[0, 4:5, :]
    ja = mbuf[0, 5:6, :]
    jb = mbuf[0, 6:7, :]

    def inject(current, finish):
        vals = dot(jnp.broadcast_to(current, (8, 128)) * own, spread)
        for k in range(8):
            h, pair = k // 4, 2 * (k % 4)
            block = dot_t(rt[k] * vals[k : k + 1, :], lt[k])
            for n in range(2):
                rows = block[32 * n : 32 * n + 32]
                bsrc[h, pair + n] = rows * rdiag[h, pair + n] if finish else rows

    def field(f, yf, ysend, s_sem, r_sem):
        def x_copies(par):
            return [
                remote(f.at[par, pl.ds(1, 2), 8], f.at[par, pl.ds(1 + x_last, 2), 0],
                       s_sem.at[par, 0], r_sem.at[par, 0], dev(xn, y, z, c)),
                remote(f.at[par, pl.ds(1, 2), 1], f.at[par, pl.ds(1 - x_first, 2), 9],
                       s_sem.at[par, 1], r_sem.at[par, 1], dev(xp, y, z, c)),
            ]

        def y_copies(par):
            return [
                remote(ysend.at[par, 0], yf.at[par, 0], s_sem.at[par, 2], r_sem.at[par, 2], dev(x, yn, z, c)),
                remote(ysend.at[par, 1], yf.at[par, 1], s_sem.at[par, 3], r_sem.at[par, 3], dev(x, yp, z, c)),
            ]

        def edge_rows(par, h, p, v):
            ysend[par, 0, h, p : p + 1, :] = v[31:32]
            ysend[par, 1, h, p : p + 1, :] = v[0:1]

        def begin():
            for copy in x_copies(0):
                copy.start()
            for h in range(2):
                for p in range(8):
                    edge_rows(0, h, p, f[0, 1 + h, p + 1])
            start_y(y_copies(0))

        def end(par=0):
            wait_y(y_copies(par))
            for copy in x_copies(par):
                copy.wait()

        def sweep(par):
            new = 1 - par

            def plane(h, p):
                v = f[par, 1 + h, p + 1]
                ylow, yhigh = shift_y(v, yf[par, 0, h, p : p + 1, :], yf[par, 1, h, p : p + 1, :])
                out = coef[0, h, p] * f[par, 1 + h, p + 2] + coef[1, h, p] * f[par, 1 + h, p]
                out = out + (coef[2, h, p] * yhigh + coef[3, h, p] * ylow)
                out = out + (coef[4, h, p] * pltpu.roll(v, 127, 1) + coef[5, h, p] * pltpu.roll(v, 1, 1))
                out = (0.2 * v + bsrc[h, p]) + out
                f[new, 1 + h, p + 1] = out
                edge_rows(new, h, p, out)

            end(par)
            for p in (0, 7):
                for h in range(2):
                    plane(h, p)
            for copy in x_copies(new):
                copy.start()
            for h in range(2):
                for p in range(1, 7):
                    plane(h, p)
            start_y(y_copies(new))

        def two(s, carry):
            sweep(0)
            sweep(1)
            return carry

        def sweeps():
            lax.fori_loop(0, RELAX_SWEEPS // 2, two, 0)

        return begin, sweeps, end

    own_lane = iota((1, 128), 1)
    own_ids = ((own_lane // 64) * 256 + x * 64 + own_lane % 64).astype(F32)
    inject(4.0 * (jnp.where(own_ids == ja, 1.0, 0.0) - jnp.where(own_ids == jb, 1.0, 0.0)), False)

    p_begin, p_sweeps, p_end = field(pf, ypf, ypsend, p_s, p_r)
    a_begin, a_sweeps, a_end = field(af, yaf, yasend, a_s, a_r)
    arrived(pf.at[0, pl.ds(1, 2), pl.ds(1, 8)], sw_r.at[0])
    p_begin()
    tile_copy.wait()
    for cc in range(2):
        for d, copy in enumerate(sg_x(cc)):
            copy.wait_send()
            arrived(sg.at[1, 0], sg_r.at[d, cc])

        @pl.when(y < 3)
        def _():
            sg_y(cc)[0].wait_send()
            arrived(yss.at[0], sg_r.at[3, cc])

        @pl.when(y > 0)
        def _():
            sg_y(cc)[1].wait_send()
            arrived(yss.at[0], sg_r.at[2, cc])

    def faces_of(h, p):
        s = sg[1 + h, p + 1]
        low = ysg[0, 0, h, p : p + 1, :]
        high = ysg[1, 0, h, p : p + 1, :]
        _, syp = shift_y(s, low, high)
        szp = jnp.where(lane == 127, 0.0, pltpu.roll(s, 127, 1))
        ux = harmonic(s, sg[1 + h, p + 2])
        uy = harmonic(s, syp)
        uz = harmonic(s, szp)
        return s, low, ux, uy, uz

    for h in range(2):
        lx = harmonic(sg[1 + h, 0], sg[1 + h, 1])
        for p in range(8):
            s, low, ux, uy, uz = faces_of(h, p)
            ly = jnp.where(row == 0, harmonic(low, s[0:1]), pltpu.roll(uy, 1, 0))
            lz = pltpu.roll(uz, 1, 1)
            r = 0.8 / (ux + lx + uy + ly + uz + lz)
            rdiag[h, p] = r
            bsrc[h, p] = bsrc[h, p] * r
            for k, face in enumerate((ux, lx, uy, ly, uz, lz)):
                coef[k, h, p] = face * r
            lx = ux

    def electrode_ids(x_):
        j = iota((128, 128), 0)
        return ((j // 64) * 256 + x_ * 64 + j % 64).astype(F32)

    p_sweeps()

    for k in range(8):
        h, pair = k // 4, 2 * (k % 4)
        block = pf[0, 1 + h, pl.ds(1 + pair, 2)].reshape(64, 128)
        vb[k : k + 1, :] = jnp.sum(rt[k] * dot(block, lt[k]), axis=0, keepdims=True)
    part = jnp.sum(dot_t(vb[...], spread) * own, axis=0, keepdims=True)
    vsend[...] = jnp.broadcast_to(part, (8, 128))

    def v_copy(k):
        xt = (x + k // 4) % 4
        yt = (y + k % 4) % 4
        return remote(vsend, vall.at[x * 4 + y], v_s.at[k], v_r, dev(xt, yt, z, c))

    for k in range(1, 16):
        v_copy(k).start()
    pltpu.make_async_copy(vsend, vall.at[x * 4 + y], v_r).start()
    arrived(af.at[0, pl.ds(1, 2), pl.ds(1, 8)], sw_r.at[1])
    a_begin()
    arrived(vall, v_r)

    def selector(x_):
        ids = electrode_ids(x_)
        return jnp.where(ids == r0, 1.0, 0.0) - jnp.where(ids == r1, 1.0, 0.0)

    readings = jnp.zeros((8, 128), F32)
    for k in range(4):
        volts = vall[4 * k] + vall[4 * k + 1] + vall[4 * k + 2] + vall[4 * k + 3]
        readings = readings + dot(volts, selector(k))
    rsend[...] = readings
    survey = (1 + zh + zl // 4) % 2

    def read_copies():
        return [
            remote(rsend, rdin.at[survey], rd_s.at[half], rd_r, dev(x, y, half * 8 + (zl + 4) % 8, c))
            for half in range(2)
        ]

    for copy in read_copies():
        copy.start()
    inject(dot_t(readings - measured, selector(x))[0:1], True)
    a_sweeps()
    p_end()
    a_end()

    def terms(h, p):
        _, _, ux, uy, uz = faces_of(h, p)
        pv = pf[0, 1 + h, p + 1]
        av = af[0, 1 + h, p + 1]
        _, py = shift_y(pv, pv[0:1], ypf[0, 1, h, p : p + 1, :])
        _, ay = shift_y(av, av[0:1], yaf[0, 1, h, p : p + 1, :])
        out = ux * (pf[0, 1 + h, p + 2] - pv) * (af[0, 1 + h, p + 2] - av)
        out = out + uy * (py - pv) * (ay - av)
        out = out + uz * (pltpu.roll(pv, 127, 1) - pv) * (pltpu.roll(av, 127, 1) - av)
        return -out

    def other(p):
        return remote(gbuf.at[p], grx.at[p], gx_s.at[p], gx_r.at[p], dev(x, y, z, 1 - c))

    def rs_copy(k, local):
        p, rh = k // 2, k % 2
        src = gsum.at[p, pl.ds(16 * rh, 16)]
        dst = rsbuf.at[z]
        if local:
            return pltpu.make_async_copy(src, dst, rs_r)
        return remote(src, dst, rs_s.at[k], rs_r, dev(x, y, 8 * c + p, rh))

    def rs_self(k):
        return (z == 8 * c + k // 2) & (c == k % 2)

    for p in range(8):
        gbuf[p] = terms(1 - c, p)
        other(p).start()
    for p in range(8):
        mine = terms(c, p)
        other(p).wait()
        gsum[p] = mine + grx[p]
        for k in (2 * p, 2 * p + 1):
            @pl.when(jnp.logical_not(rs_self(k)))
            def _():
                rs_copy(k, False).start()

            @pl.when(rs_self(k))
            def _():
                rs_copy(k, True).start()

    arrived(rsbuf, rs_r)
    added = rsbuf[0]
    for k in range(1, 16):
        added = added + rsbuf[k]
    osum[...] = added

    def ag_copy(k, local):
        dst = grad.at[zl % 2, pl.ds(pl.multiple_of(32 * y + 16 * c, 16), 16)]
        if local:
            return pltpu.make_async_copy(osum, dst, ag_r)
        return remote(osum, dst, ag_s.at[k], ag_r, dev(x, zl // 2, 8 * zh + ag_z(k), k % 2))

    def ag_z(k):
        return (k // 2) * (zl // 4) + (7 - k // 2) * (1 - zl // 4)

    def ag_self(k):
        return (y == zl // 2) & (zl == ag_z(k)) & (c == k % 2)

    for k in range(16):
        @pl.when(jnp.logical_not(ag_self(k)))
        def _():
            ag_copy(k, False).start()

        @pl.when(ag_self(k))
        def _():
            ag_copy(k, True).start()

    arrived(rdin, rd_r)
    read[0:1, :] = rdin[0, 0:1, 0:64]
    read[1:2, :] = rdin[1, 0:1, 0:64]
    arrived(grad, ag_r)

    @pl.when(home)
    def _():
        for a in range(5):
            for d in range(1, 4):
                in_copy(a, d).wait_send()

            @pl.when(leaving)
            def _():
                for d in range(4):
                    out_copy(a, d).wait_send()


    for which in range(3):
        for j in range(2):
            for copy in swap_copies(which, j):
                copy.wait_send()
    for k in range(1, 16):
        v_copy(k).wait_send()
    for copy in read_copies():
        copy.wait_send()
    for k in range(16):
        @pl.when(jnp.logical_not(rs_self(k)))
        def _():
            rs_copy(k, False).wait_send()

        @pl.when(jnp.logical_not(ag_self(k)))
        def _():
            ag_copy(k, False).wait_send()


def on_device(
    concentration, velocity, porosity, contacts, sources, receivers, observed, potential_init, adjoint_init
):
    V = pltpu.VMEM
    D = pltpu.SemaphoreType.DMA
    scratch = [
        V((2, 12, 32, 128), F32), V((2, 2, 2, 8, 128), F32), V((2, 2, 8, 128), F32), V((4, 8, 32, 128), F32),
        V((4, 10, 32, 128), F32), V((2, 2, 2, 8, 128), F32), V((2, 8, 128), F32),
        V((6, 2, 8, 32, 128), F32), V((2, 8, 32, 128), F32), V((2, 8, 32, 128), F32),
        V((2, 4, 10, 32, 128), F32), V((2, 2, 2, 8, 128), F32), V((2, 2, 2, 8, 128), F32),
        V((2, 4, 10, 32, 128), F32), V((2, 2, 2, 8, 128), F32), V((2, 2, 2, 8, 128), F32),
        V((8, 8, 128), F32), V((8, 64, 128), F32), V((8, 128, 128), BF16), V((8, 128), F32), V((8, 128), F32),
        V((16, 8, 128), F32), V((8, 128), F32), V((2, 8, 128), F32),
        V((8, 32, 128), F32), V((8, 32, 128), F32), V((8, 32, 128), F32), V((16, 16, 128), F32), V((16, 128), F32),
        V((3, 2, 128, 128), BF16), V((3, 2, 128, 128), F32), V((4, 16), jnp.int32), V((2, 2), jnp.int32),
        V((2, 2, 64), jnp.int32), V((2, 64), F32), V((2, 8, 128), F32),
        D((5, 4)), D((5, 4)), D((5, 2)), D((5, 2)), D((2, 4)), D((2, 4)), D((3, 2, 4)), D((3,)), D((4, 2)), D((4, 2)), D, D,
        D((2, 4)), D((2, 4)), D((2, 4)), D((2, 4)), D((16,)), D, D((2,)), D, D((8,)), D((8,)), D((16,)), D, D((16,)), D,
        D((5,)),
    ]
    gradient, readings = pl.pallas_call(
        kernel,
        out_shape=(jax.ShapeDtypeStruct((2, 128, 128), F32), jax.ShapeDtypeStruct((2, 64), F32)),
        in_specs=[pl.BlockSpec(memory_space=pl.ANY)] * 9,
        out_specs=(pl.BlockSpec(memory_space=pltpu.VMEM), pl.BlockSpec(memory_space=pltpu.VMEM)),
        scratch_shapes=scratch,
        compiler_params=pltpu.CompilerParams(collective_id=0, has_side_effects=True),
        name="survey_gradient",
    )(
        concentration, velocity, porosity, contacts.T, sources, jnp.swapaxes(receivers, 1, 2), observed,
        potential_init, adjoint_init,
    )
    return gradient, readings


def solution(mesh):
    return jax.shard_map(
        on_device,
        mesh=mesh,
        in_specs=(
            P("space", None, None),
            P(None, "space", None, None),
            P("space", None, None),
            P("space", None),
            P("tm", None),
            P("tm", None, None),
            P("tm", None),
            P("tm", "space", None, None),
            P("tm", "space", None, None),
        ),
        out_specs=(P("space", None, None), P("tm", None)),
        check_vma=False,
    )
```
